128 devices in a mesh: slab: 8 (over x, core), col: 16 (over z, y).
Axes of the slice: x: 4, y: 4, z: 4, core: 2. Of those that a mesh axis runs over, the one named last changes fastest.
Arguments:
- modes: float32 [64, 393216], P(None, ('slab', 'col')), may hold values from -20 to 20
- tiles: bfloat16 [3072, 384, 384], P(('slab', 'col')), may hold values from -0.0625 to 0.0625
- tile_pair: int32 [3072], P(('slab', 'col')), may hold values from 0 to 23, as said below
- boundary: int32 [128, 2], P(('slab', 'col')), may hold values from 96 to 384, as said below
Outputs:
- filtered: float32 [64, 393216], P(None, ('slab', 'col'))
The draws below stay inside these ranges and needn't reach their ends.
Inputs may be any that keep to these rules, and one draw needn't show every extreme that they name: `tile_pair`: each row block's 24 entries hold every number of 0 to 23 once. `boundary`: on each side, some row block reaches 384 in every draw.
All inputs are finite; a program needn't handle non-finite values.
Results may differ from the reference program's by a relative error of at most 0.0059.
Values may be sent and summed in bfloat16 or wider, within the bound.
No kernel may reach another device: no remote copies, remote signals or barrier semaphores. Data moves between devices by JAX's collectives and lax.ppermute only.
A program may use at most 64 MiB of HBM per device.

```python
import jax
import jax.numpy as jnp
from jax import lax

K = 64
TB = 384
RTG = 8
DEG = 8
APPS = 1
TL = 24
BLOCKS = 128
NROWS = 393216
TILES = 3072


def draw_modes(key, part):
    row_ramp = jnp.exp(jnp.log(3.0) * jnp.arange(NROWS, dtype=jnp.float32) / NROWS)
    base_values = jnp.clip(jax.random.normal(key, (K, NROWS), jnp.float32), -6.0, 6.0)
    return base_values * row_ramp[None, :]


def draw_tile_pair(key, part):
    block_count = TILES // TL
    raw_scores = jax.random.randint(key, (block_count, TL), 0, 65536)
    scores = raw_scores * TL + jnp.arange(TL, dtype=jnp.int32)[None, :]
    return jnp.argsort(scores, axis=1).astype(jnp.int32).reshape(TILES)


def draw_boundary(key, part):
    counts = jax.random.randint(key, (BLOCKS, 2), TB // 4, TB + 1)
    lower_full = jax.random.randint(jax.random.fold_in(key, 11), (), 0, BLOCKS)
    upper_full = jax.random.randint(jax.random.fold_in(key, 13), (), 0, BLOCKS)
    counts = counts.at[lower_full, 0].set(TB)
    counts = counts.at[upper_full, 1].set(TB)
    return counts.astype(jnp.int32)


def block_scale(rng, shape, pieces, least, top_value):
    def one(axis_at, shards_of):
        steps = jax.random.uniform(jax.random.fold_in(jax.random.fold_in(rng, 6), axis_at), (shards_of,), jnp.float32, least / len(pieces), top_value / len(pieces))
        return jnp.repeat(jnp.exp(steps), shape[axis_at] // shards_of).reshape((-1,) + (1,) * (len(shape) - axis_at - 1))

    level = one(*pieces[0])
    for cut in pieces[1:]:
        level = level * one(*cut)
    return level


def bell_draw(key, dims, deviation, reach, split=(), kind=jnp.bfloat16):
    values = jax.random.normal(key, dims, jnp.float32) * deviation
    if len(split) > 0:
        values = block_scale(key, dims, split, -0.22, 0.18) * values
    return jnp.clip(values, min=-reach, max=reach).astype(kind)


def setup_inputs(seed: int = 0) -> dict:
    arg_keys = jax.random.split(jax.random.key(seed), 5)
    return {
        "modes": draw_modes(jax.random.fold_in(arg_keys[4], 71), 0),
        "tiles": bell_draw(arg_keys[1], (TILES, TB, TB), (24 * TB) ** -0.5, 0.0625, ((0, 128),)),
        "tile_pair": draw_tile_pair(jax.random.fold_in(arg_keys[4], 71), 0),
        "boundary": draw_boundary(jax.random.fold_in(arg_keys[4], 71), 0),
    }


center = 0.25

def apply_hessian(xbf, tiles, tile_pair, boundary):
    mode_count = xbf.shape[0]
    blocks_x = jnp.transpose(xbf.reshape(mode_count, BLOCKS, RTG, TB), (1, 0, 2, 3))
    columns_at = jnp.arange(TB, dtype=jnp.int32)
    keep_lower = columns_at[None, :] < boundary[:, 0][:, None]
    keep_upper = columns_at[None, :] >= (TB - boundary[:, 1])[:, None]
    lower_edge = jnp.where(keep_lower[:, None, :], blocks_x[:, :, 0], jnp.zeros_like(blocks_x[:, :, 0]))
    upper_edge = jnp.where(keep_upper[:, None, :], blocks_x[:, :, RTG - 1], jnp.zeros_like(blocks_x[:, :, 0]))
    variants = jnp.concatenate([blocks_x, lower_edge[:, :, None], upper_edge[:, :, None]], axis=2)
    tiles_b = tiles.reshape(BLOCKS, TL, TB, TB)
    pairs_b = tile_pair.reshape(BLOCKS, TL)

    def one_block(args):
        varied, weights, pairs = args
        column_tile = pairs // 3
        offset = pairs % 3 - 1
        chosen_slot = jnp.where((offset == -1) & (column_tile == 0), RTG, jnp.where((offset == 1) & (column_tile == RTG - 1), RTG + 1, column_tile))
        chosen = jnp.take(varied, chosen_slot, axis=1)
        product = jnp.einsum('ktc,tcr->ktr', chosen.astype(jnp.float32), weights.astype(jnp.float32))
        target = column_tile + offset + 1
        onehot = (target[:, None] == jnp.arange(RTG + 2, dtype=jnp.int32)[None, :]).astype(jnp.float32)
        return jnp.einsum('ktr,ti->kir', product, onehot)
    spread_out = lax.map(one_block, (variants, tiles_b, pairs_b))
    own_rows = spread_out[:, :, 1:RTG + 1]
    from_below = jnp.roll(spread_out[:, :, RTG + 1], 1, axis=0)
    from_above = jnp.roll(spread_out[:, :, 0], -1, axis=0)
    own_rows = own_rows.at[:, :, 0].add(from_below)
    own_rows = own_rows.at[:, :, RTG - 1].add(from_above)
    return jnp.transpose(own_rows, (1, 0, 2, 3)).reshape(mode_count, NROWS)

def reference(modes, tiles, tile_pair, boundary):

    def mapped(field):
        return apply_hessian(field.astype(jnp.bfloat16), tiles, tile_pair, boundary) - center * field
    current_block = modes
    for app_index in range(APPS):
        previous = current_block
        current = mapped(current_block)
        for step_index in range(DEG - 1):
            following = 2.0 * mapped(current) - previous
            previous = current
            current = following
        gram = jnp.dot(current.astype(jnp.float32), current.T.astype(jnp.float32), precision=lax.Precision.HIGHEST, preferred_element_type=jnp.float32) / NROWS
        factor = jnp.linalg.cholesky(gram)
        current_block = jax.scipy.linalg.solve_triangular(factor, current, lower=True)
    return current_block
```

```python
import functools

import jax
import jax.numpy as jnp
from jax import lax
from jax.experimental import pallas as pl
from jax.experimental.pallas import tpu as pltpu
from jax.sharding import PartitionSpec as P

DEG = 8
center = 0.25
AXES = ("slab", "col")
K = 64
TB = 384
RT = 8
TL = 24
ROWS = RT * TB
F32 = jnp.float32
BF16 = jnp.bfloat16

VM = pl.BlockSpec(memory_space=pltpu.VMEM)
SM = pl.BlockSpec(memory_space=pltpu.SMEM)
ANY = pl.BlockSpec(memory_space=pl.ANY)


def vmem(shape, dtype):
    return pltpu.VMEM(shape, dtype)


def pin(x):
    return pltpu.with_memory_space_constraint(x, pltpu.VMEM)


def params(mib):
    return pltpu.CompilerParams(vmem_limit_bytes=mib << 20)


def target_columns(r):
    return max(r - 1, 0) * TB, min(r + 2, RT) * TB


def target_rows(r):
    start = 0 if r == 0 else (3 * r - 1)
    return start * TB, (start + (2 if r in (0, RT - 1) else 3)) * TB


def target_pairs(r):
    return [3 * c + (r - c) + 1 for c in (r - 1, r, r + 1) if 0 <= c < RT]


def dot(a, b):
    return jnp.dot(a, b, preferred_element_type=F32)


def overflow(low, high, we_ref, bound_ref, par_ref, se_ref, so_ref):
    column = lax.broadcasted_iota(jnp.int32, (K, TB), 1)
    low = jnp.where(column < bound_ref[0, 0], low, 0.0).astype(BF16)
    high = jnp.where(column >= TB - bound_ref[0, 1], high, 0.0).astype(BF16)
    s_low = dot(low, we_ref[0]).astype(BF16)
    s_high = dot(high, we_ref[1]).astype(BF16)
    even = par_ref[0] == 0
    se_ref[...] = jnp.where(even, s_high, s_low)
    so_ref[...] = jnp.where(even, s_low, s_high)


def first_kernel(pair_ref, bound_ref, par_ref, modes_ref, tiles_ref, we_ref, ye_ref, se_ref, so_ref, sems):
    low_at = jnp.int32(0)
    high_at = jnp.int32(0)
    for t in range(TL):
        low_at = jnp.where(pair_ref[t] == 0, t, low_at)
        high_at = jnp.where(pair_ref[t] == TL - 1, t, high_at)
    copies = [
        pltpu.make_async_copy(modes_ref.at[:, pl.ds(0, TB)], ye_ref.at[:, pl.ds(0, TB)], sems.at[0]),
        pltpu.make_async_copy(tiles_ref.at[low_at], we_ref.at[0], sems.at[1]),
        pltpu.make_async_copy(modes_ref.at[:, pl.ds(ROWS - TB, TB)], ye_ref.at[:, pl.ds(TB, TB)], sems.at[2]),
        pltpu.make_async_copy(tiles_ref.at[high_at], we_ref.at[1], sems.at[3]),
    ]
    for c in copies:
        c.start()
    for c in copies:
        c.wait()
    overflow(ye_ref[:, :TB], ye_ref[:, TB:], we_ref, bound_ref, par_ref, se_ref, so_ref)


def load_kernel(pair_ref, modes_ref, tiles_ref, y0_ref, w_ref, next_ref, inv, xs, sems, msem):
    mcopy = pltpu.make_async_copy(modes_ref, y0_ref, msem)
    mcopy.start()
    for t in range(TL):
        inv[pair_ref[t]] = t
    copies = {}
    slot = 0
    for r in range(RT):
        for p in target_pairs(r):
            copies[p] = pltpu.make_async_copy(
                tiles_ref.at[inv[p]], w_ref.at[pl.ds(slot * TB, TB)], sems.at[slot]
            )
            copies[p].start()
            slot += 1
    mcopy.wait()
    xs[...] = y0_ref[...].astype(BF16)
    for r in range(RT):
        for p in target_pairs(r):
            copies[p].wait()
        c0, c1 = target_columns(r)
        w0, w1 = target_rows(r)
        here = slice(r * TB, (r + 1) * TB)
        next_ref[:, here] = dot(xs[:, c0:c1], w_ref[w0:w1]) - center * y0_ref[:, here]


def edge_kernel(factor, bound_ref, par_ref, y_ref, re_ref, ro_ref, we_ref, ye_ref, se_ref, so_ref):
    even = par_ref[0] == 0
    re, ro = re_ref[...], ro_ref[...]
    low = y_ref[:, :TB] + factor * jnp.where(even, ro, re).astype(F32)
    high = y_ref[:, ROWS - TB :] + factor * jnp.where(even, re, ro).astype(F32)
    ye_ref[:, :TB] = low
    ye_ref[:, TB:] = high
    overflow(low, high, we_ref, bound_ref, par_ref, se_ref, so_ref)


def gram(y):
    return lax.dot_general(
        y, y, (((1,), (1,)), ((), ())), precision=lax.Precision.HIGHEST, preferred_element_type=F32
    )


def step_kernel(last, y_ref, ye_ref, z_ref, ze_ref, w_ref, next_ref, *rest):
    xs = rest[-1]
    xs[:, :TB] = ye_ref[:, :TB].astype(BF16)
    xs[:, TB : ROWS - TB] = y_ref[:, TB : ROWS - TB].astype(BF16)
    xs[:, ROWS - TB :] = ye_ref[:, TB:].astype(BF16)
    for r in range(RT):
        c0, c1 = target_columns(r)
        w0, w1 = target_rows(r)
        here = slice(r * TB, (r + 1) * TB)
        if r == 0:
            y, z = ye_ref[:, :TB], ze_ref[:, :TB]
        elif r == RT - 1:
            y, z = ye_ref[:, TB:], ze_ref[:, TB:]
        else:
            y, z = y_ref[:, here], z_ref[:, here]
        next_ref[:, here] = 2.0 * (dot(xs[:, c0:c1], w_ref[w0:w1]) - center * y) - z
    if last:
        rest[0][...] = gram(next_ref[:, TB : ROWS - TB])


def final_kernel(par_ref, y_ref, re_ref, ro_ref, gi_ref, ye_ref, g_ref):
    even = par_ref[0] == 0
    re, ro = re_ref[...], ro_ref[...]
    ye_ref[:, :TB] = y_ref[:, :TB] + 2.0 * jnp.where(even, ro, re).astype(F32)
    ye_ref[:, TB:] = y_ref[:, ROWS - TB :] + 2.0 * jnp.where(even, re, ro).astype(F32)
    g = gi_ref[...] + gram(ye_ref[...])
    g_ref[...] = jnp.concatenate([g[: K // 2], g[K // 2 :]], axis=1)


def whiten_kernel(scale, g_ref, y_ref, ye_ref, out_ref):
    g = g_ref[...] * scale
    g = jnp.concatenate([g[:, :K], g[:, K:]], axis=0)
    row = lax.broadcasted_iota(jnp.int32, (K, K), 0)
    col = lax.broadcasted_iota(jnp.int32, (K, K), 1)
    eye = (row == col).astype(F32)
    whole = jnp.concatenate([g, eye], axis=1)
    blocks = [whole[8 * i : 8 * i + 8] for i in range(K // 8)]
    sub = lax.broadcasted_iota(jnp.int32, (8, 1), 0)
    for k in range(K):
        b, s = divmod(k, 8)
        pivot_row = blocks[b][s : s + 1]
        scaled = pivot_row / pivot_row[:, k : k + 1]
        for i in range(b, K // 8):
            mult = blocks[i][:, k : k + 1]
            if i == b:
                mult = jnp.where(sub > s, mult, 0.0)
            blocks[i] = blocks[i] - mult * scaled
    whole = jnp.concatenate(blocks, axis=0)
    diagonal = jnp.sum(jnp.where(row == col, whole[:, :K], 0.0), axis=1, keepdims=True)
    linv = whole[:, K:] / jnp.sqrt(diagonal)

    def apply(y):
        return jnp.dot(linv, y, precision=lax.Precision.HIGHEST, preferred_element_type=F32)

    out_ref[:, :TB] = apply(ye_ref[:, :TB])
    for r in range(1, RT - 1):
        out_ref[:, r * TB : (r + 1) * TB] = apply(y_ref[:, r * TB : (r + 1) * TB])
    out_ref[:, ROWS - TB :] = apply(ye_ref[:, TB:])


def local(modes, tiles, tile_pair, boundary):
    slabs, cols = lax.axis_size("slab"), lax.axis_size("col")
    count = slabs * cols
    parity = (lax.axis_index("col") & 1).astype(jnp.int32).reshape(1)
    pairs_even = [(i, i ^ 1) for i in range(count)]
    pairs_odd = [(i, (i + 1) % count if i % 2 else (i - 1) % count) for i in range(count)]

    def exchange(se, so):
        ro = lax.ppermute(so, AXES, pairs_odd)
        re = lax.ppermute(se, AXES, pairs_even)
        return re, ro

    send = vmem((K, TB), BF16)
    edges = vmem((K, 2 * TB), F32)
    block = vmem((K, ROWS), F32)
    we, ye, se, so = pl.pallas_call(
        first_kernel,
        out_shape=(vmem((2, TB, TB), BF16), edges, send, send),
        in_specs=[SM, SM, SM, ANY, ANY],
        out_specs=(VM, VM, VM, VM),
        scratch_shapes=[pltpu.SemaphoreType.DMA((4,))],
        compiler_params=params(8),
        name="first",
    )(tile_pair, boundary, parity, modes, tiles)
    re, ro = exchange(se, so)
    flops = 2 * K * TB * TB * 22
    y0, w, y = pl.pallas_call(
        load_kernel,
        out_shape=(block, vmem(((TL - 2) * TB, TB), BF16), block),
        in_specs=[SM, ANY, ANY],
        out_specs=(VM, VM, VM),
        scratch_shapes=[
            pltpu.SMEM((TL,), jnp.int32),
            pltpu.VMEM((K, ROWS), BF16),
            pltpu.SemaphoreType.DMA((TL - 2,)),
            pltpu.SemaphoreType.DMA,
        ],
        compiler_params=params(16),
        cost_estimate=pl.CostEstimate(flops=flops, bytes_accessed=8 << 20, transcendentals=0),
        name="load",
    )(tile_pair, modes, tiles)
    z, ze = y0, ye
    for k in range(1, DEG):
        ye, se, so = pl.pallas_call(
            functools.partial(edge_kernel, 1.0 if k == 1 else 2.0),
            out_shape=(edges, send, send),
            in_specs=[SM, SM, VM, VM, VM, VM],
            out_specs=(VM, VM, VM),
            compiler_params=params(8),
            name="edge",
        )(boundary, parity, pin(y), re, ro, pin(we))
        re, ro = exchange(se, so)
        last = k == DEG - 1
        outs = pl.pallas_call(
            functools.partial(step_kernel, last),
            out_shape=(block, vmem((K, K), F32)) if last else block,
            in_specs=[VM] * 5,
            out_specs=(VM, VM) if last else VM,
            scratch_shapes=[pltpu.VMEM((K, ROWS), BF16)],
            compiler_params=params(12),
            cost_estimate=pl.CostEstimate(flops=flops, bytes_accessed=8 << 20, transcendentals=0),
            name="step",
        )(pin(y), pin(ye), pin(z), pin(ze), pin(w))
        z, ze = y, ye
        if last:
            y, gi = outs
        else:
            y = outs
    ye, g = pl.pallas_call(
        final_kernel,
        out_shape=(edges, vmem((K // 2, 2 * K), F32)),
        in_specs=[SM, VM, VM, VM, VM],
        out_specs=(VM, VM),
        compiler_params=params(8),
        name="final",
    )(parity, pin(y), re, ro, pin(gi))
    stride = 1
    for axis_bits in ((1, 3), (4, 12), (16,), (32, 96)):
        for bits in axis_bits:
            g = g + lax.ppermute(g, AXES, [(i, i ^ bits) for i in range(count)])
    return pl.pallas_call(
        functools.partial(whiten_kernel, 1.0 / (ROWS * count)),
        out_shape=jax.ShapeDtypeStruct((K, ROWS), F32),
        in_specs=[VM, VM, VM],
        out_specs=VM,
        compiler_params=params(16),
        name="whiten",
    )(g, pin(y), pin(ye))


def solution(mesh):
    placed = (
        P(None, AXES),
        P(AXES, None, None),
        P(AXES),
        P(AXES, None),
    )
    return jax.shard_map(
        local, mesh=mesh, in_specs=placed, out_specs=P(None, AXES), check_vma=False
    )
```

```python
import functools

import jax
import jax.numpy as jnp
from jax import lax
from jax.experimental import pallas as pl
from jax.experimental.pallas import tpu as pltpu
from jax.sharding import PartitionSpec as P

DEG = 8
center = 0.25
AXES = ("slab", "col")
K = 64
TB = 384
RT = 8
TL = 24
ROWS = RT * TB
F32 = jnp.float32
BF16 = jnp.bfloat16

VM = pl.BlockSpec(memory_space=pltpu.VMEM)
SM = pl.BlockSpec(memory_space=pltpu.SMEM)
HBM = pl.BlockSpec(memory_space=pltpu.HBM)


def pin(x):
    return pltpu.with_memory_space_constraint(x, pltpu.VMEM)


def hbm(x):
    return pltpu.with_memory_space_constraint(x, pltpu.HBM)


def params(mib):
    return pltpu.CompilerParams(vmem_limit_bytes=mib << 20)


def cost(tile_products):
    return pl.CostEstimate(flops=2 * K * TB * TB * tile_products, bytes_accessed=8 << 20, transcendentals=0)


def dot(a, b):
    return jnp.dot(a, b, preferred_element_type=F32)


def tile(i, n=1):
    return slice(i * TB, (i + n) * TB)


OUTER = [1, 3, 20, 22]
INNER = [3 * c + (r - c) + 1 for r in range(1, RT - 1) for c in (r - 1, r, r + 1)]


def inner(r, first=0, count=3):
    return tile(3 * (r - 1) + first, count)


def first_kernel(
    bound_ref, par_ref, pair_ref, modes_ref, tiles_ref,
    outer_ref, we_ref, z_ref, se_ref, so_ref, inv_ref,
    pair, bound, ym, sems, ssem,
):
    to_smem = pltpu.make_async_copy(pair_ref, pair, ssem.at[0])
    to_smem.start()
    bound_copy = pltpu.make_async_copy(bound_ref, bound, ssem.at[1])
    bound_copy.start()
    modes = [
        pltpu.make_async_copy(modes_ref.at[:, tile(0, 2)], ym.at[:, tile(0, 2)], sems.at[6]),
        pltpu.make_async_copy(modes_ref.at[:, tile(6, 2)], ym.at[:, tile(2, 2)], sems.at[7]),
    ]
    for c in modes:
        c.start()
    to_smem.wait()
    for t in range(TL):
        inv_ref[pair[t]] = t
    copies = [
        pltpu.make_async_copy(tiles_ref.at[inv_ref[p]], outer_ref.at[tile(i)], sems.at[i])
        for i, p in enumerate(OUTER)
    ] + [
        pltpu.make_async_copy(tiles_ref.at[inv_ref[p]], we_ref.at[tile(i)], sems.at[4 + i])
        for i, p in enumerate((0, TL - 1))
    ]
    for c in copies:
        c.start()
    bound_copy.wait()
    for c in modes + copies:
        c.wait()
    row = lax.broadcasted_iota(jnp.int32, (TB, TB), 0)
    zero = jnp.zeros((TB, TB), BF16)
    w_low = jnp.where(row < bound[0, 0], we_ref[tile(0)], zero)
    w_high = jnp.where(row >= TB - bound[0, 1], we_ref[tile(1)], zero)
    we_ref[tile(0)] = w_low
    we_ref[tile(1)] = w_high
    xs = ym[...].astype(BF16)
    z_low = dot(xs[:, tile(0, 2)], outer_ref[tile(0, 2)]) - center * ym[:, tile(0)]
    z_high = dot(xs[:, tile(2, 2)], outer_ref[tile(2, 2)]) - center * ym[:, tile(3)]
    z_ref[:, tile(0)] = z_low
    z_ref[:, tile(1)] = z_high
    even = par_ref[0] == 0
    send(even, xs[:, tile(0)], xs[:, tile(3)], z_low, z_high, se_ref, so_ref)
    se_ref[2 * K :] = jnp.where(even, w_high, w_low)
    so_ref[2 * K :] = jnp.where(even, w_low, w_high)


def send(even, x_low, x_high, z_low, z_high, se_ref, so_ref):
    z_low, z_high = z_low.astype(BF16), z_high.astype(BF16)
    se_ref[:K] = jnp.where(even, x_high, x_low)
    se_ref[K : 2 * K] = jnp.where(even, z_high, z_low)
    so_ref[:K] = jnp.where(even, x_low, x_high)
    so_ref[K : 2 * K] = jnp.where(even, z_low, z_high)


def interior(factor, previous, xs, ys, w_in, w_out, w_edge, j_ref, i_ref, b_ref, o_ref, xn):
    for r in range(1, RT - 1):
        acc = dot(xs[:, tile(r - 1, 3)], w_in[inner(r)]) - center * ys(r)
        nxt = acc if previous is None else factor * acc - previous(r)
        j_ref[:, tile(r - 1)] = nxt
        xn[:, tile(r - 1)] = nxt.astype(BF16)
    o_ref[:, tile(0)] = factor * dot(xs[:, tile(0)], w_edge[tile(0)])
    o_ref[:, tile(1)] = factor * dot(xs[:, tile(RT - 1)], w_edge[tile(1)])
    for r in range(2, RT - 2):
        acc = dot(xn[:, tile(r - 2, 3)], w_in[inner(r)]) - center * j_ref[:, tile(r - 1)]
        i_ref[:, tile(r - 2)] = 2.0 * acc - ys(r)
    b_ref[:, tile(0)] = 2.0 * dot(xn[:, tile(0)], w_out[tile(1)]) - ys(0)
    acc = dot(xn[:, tile(0, 2)], w_in[inner(1, 1, 2)]) - center * j_ref[:, tile(0)]
    b_ref[:, tile(1)] = 2.0 * acc - ys(1)
    acc = dot(xn[:, tile(4, 2)], w_in[inner(6, 0, 2)]) - center * j_ref[:, tile(5)]
    b_ref[:, tile(2)] = 2.0 * acc - ys(6)
    b_ref[:, tile(3)] = 2.0 * dot(xn[:, tile(5)], w_out[tile(2)]) - ys(7)


def load_kernel(
    inv_ref, modes_ref, tiles_ref, w_out, w_edge,
    w_in, j_ref, i_ref, b_ref, o_ref,
    y0, xs, xn, sems, msem,
):
    mcopy = pltpu.make_async_copy(modes_ref, y0, msem)
    mcopy.start()
    copies = [
        pltpu.make_async_copy(tiles_ref.at[inv_ref[p]], w_in.at[tile(i)], sems.at[i])
        for i, p in enumerate(INNER)
    ]
    for c in copies:
        c.start()
    mcopy.wait()
    for c in copies:
        c.wait()
    xs[...] = y0[...].astype(BF16)
    interior(1.0, None, xs, lambda r: y0[:, tile(r)], w_in, w_out, w_edge, j_ref, i_ref, b_ref, o_ref, xn)


def step_kernel(last, e_ref, m_ref, z_ref, w_in, w_out, w_edge, j_ref, i_ref, b_ref, o_ref, *rest):
    xs, xn = rest[-2:]
    xs[:, tile(0, 2)] = e_ref[:, tile(0, 2)].astype(BF16)
    xs[:, tile(2, 4)] = m_ref[...].astype(BF16)
    xs[:, tile(6, 2)] = e_ref[:, tile(2, 2)].astype(BF16)

    def ys(r):
        if r < 2:
            return e_ref[:, tile(r)]
        if r >= RT - 2:
            return e_ref[:, tile(r - 4)]
        return m_ref[:, tile(r - 2)]

    interior(
        2.0, lambda r: z_ref[:, tile(r - 1)], xs, ys, w_in, w_out, w_edge, j_ref, i_ref, b_ref, o_ref, xn
    )
    if last:
        rest[0][...] = gram(i_ref[...])


def gram(y):
    return lax.dot_general(
        y, y, (((1,), (1,)), ((), ())), precision=lax.Precision.HIGHEST, preferred_element_type=F32
    )


def edges(factor, even, re_ref, ro_ref, z_ref, o_ref, b_ref, w_in, w_out, w_low, w_high):
    re, ro = re_ref[: 2 * K], ro_ref[: 2 * K]
    low, high = jnp.where(even, ro, re), jnp.where(even, re, ro)
    y_low = z_ref[:, tile(0)] + factor * dot(low[:K], w_low)
    y_high = z_ref[:, tile(1)] + factor * dot(high[:K], w_high)
    far_low = (low[K:].astype(F32) + o_ref[:, tile(0)]).astype(BF16)
    far_high = (high[K:].astype(F32) + o_ref[:, tile(1)]).astype(BF16)
    x_low, x_high = y_low.astype(BF16), y_high.astype(BF16)
    acc = dot(far_low, w_low) + dot(x_low, w_out[tile(0)]) - center * y_low
    e0 = b_ref[:, tile(0)] + 2.0 * acc
    acc = dot(far_high, w_high) + dot(x_high, w_out[tile(3)]) - center * y_high
    e3 = b_ref[:, tile(3)] + 2.0 * acc
    e1 = b_ref[:, tile(1)] + 2.0 * dot(x_low, w_in[inner(1, 0, 1)])
    e2 = b_ref[:, tile(2)] + 2.0 * dot(x_high, w_in[inner(6, 2, 1)])
    return y_low, y_high, (e0, e1, e2, e3)


def edge_kernel(
    at_first, par_ref, re_ref, ro_ref, z_ref, o_ref, b_ref, w_in, w_out, *rest
):
    even = par_ref[0] == 0
    if at_first:
        e_ref, zn_ref, se_ref, so_ref, wn_ref = rest
        we, wo = re_ref[2 * K :], ro_ref[2 * K :]
        w_low, w_high = jnp.where(even, wo, we), jnp.where(even, we, wo)
        wn_ref[tile(0)] = w_low
        wn_ref[tile(1)] = w_high
    else:
        wn_ref, e_ref, zn_ref, se_ref, so_ref = rest
    w_low, w_high = wn_ref[tile(0)], wn_ref[tile(1)]
    y_low, y_high, e = edges(
        1.0 if at_first else 2.0, even, re_ref, ro_ref, z_ref, o_ref, b_ref, w_in, w_out, w_low, w_high
    )
    for i in range(4):
        e_ref[:, tile(i)] = e[i]
    x = [v.astype(BF16) for v in e]
    z_low = 2.0 * (dot(x[0], w_out[tile(0)]) + dot(x[1], w_out[tile(1)]) - center * e[0]) - y_low
    z_high = 2.0 * (dot(x[2], w_out[tile(2)]) + dot(x[3], w_out[tile(3)]) - center * e[3]) - y_high
    zn_ref[:, tile(0)] = z_low
    zn_ref[:, tile(1)] = z_high
    send(even, x[0], x[3], z_low, z_high, se_ref, so_ref)


def final_kernel(par_ref, re_ref, ro_ref, z_ref, o_ref, b_ref, w_in, w_out, wn_ref, gi_ref, e_ref, g_ref):
    even = par_ref[0] == 0
    w_low, w_high = wn_ref[tile(0)], wn_ref[tile(1)]
    _, _, e = edges(2.0, even, re_ref, ro_ref, z_ref, o_ref, b_ref, w_in, w_out, w_low, w_high)
    for i in range(4):
        e_ref[:, tile(i)] = e[i]
    g = gi_ref[...] + gram(e_ref[...])
    g_ref[...] = jnp.concatenate([g[: K // 2], g[K // 2 :]], axis=1)


def whiten_kernel(scale, g_ref, e_ref, i_ref, out_ref):
    g = g_ref[...] * scale
    g = jnp.concatenate([g[:, :K], g[:, K:]], axis=0)
    row = lax.broadcasted_iota(jnp.int32, (K, K), 0)
    col = lax.broadcasted_iota(jnp.int32, (K, K), 1)
    eye = (row == col).astype(F32)
    whole = jnp.concatenate([g, eye], axis=1)
    blocks = [whole[8 * i : 8 * i + 8] for i in range(K // 8)]
    sub = lax.broadcasted_iota(jnp.int32, (8, 1), 0)
    for k in range(K):
        b, s = divmod(k, 8)
        pivot_row = blocks[b][s : s + 1]
        scaled = pivot_row / pivot_row[:, k : k + 1]
        for i in range(b, K // 8):
            mult = blocks[i][:, k : k + 1]
            if i == b:
                mult = jnp.where(sub > s, mult, 0.0)
            blocks[i] = blocks[i] - mult * scaled
    whole = jnp.concatenate(blocks, axis=0)
    diagonal = jnp.sum(jnp.where(row == col, whole[:, :K], 0.0), axis=1, keepdims=True)
    linv = whole[:, K:] / jnp.sqrt(diagonal)

    def apply(y):
        return jnp.dot(linv, y, precision=lax.Precision.HIGHEST, preferred_element_type=F32)

    out_ref[:, tile(0, 2)] = apply(e_ref[:, tile(0, 2)])
    out_ref[:, tile(2, 4)] = apply(i_ref[...])
    out_ref[:, tile(6, 2)] = apply(e_ref[:, tile(2, 2)])


def local(modes, tiles, tile_pair, boundary):
    count = lax.axis_size("slab") * lax.axis_size("col")
    parity = (lax.axis_index("col") & 1).astype(jnp.int32).reshape(1)
    pairs_even = [(i, i ^ 1) for i in range(count)]
    pairs_odd = [(i, (i + 1) % count if i % 2 else (i - 1) % count) for i in range(count)]

    def exchange(se, so):
        ro = lax.ppermute(so, AXES, pairs_odd)
        re = lax.ppermute(se, AXES, pairs_even)
        return re, ro

    def f32(tiles_wide):
        return pltpu.VMEM((K, tiles_wide * TB), F32)

    def weights(n):
        return pltpu.VMEM((n * TB, TB), BF16)

    def sends(rows):
        return pltpu.VMEM((rows, TB), BF16)

    w_out, w_edge, z, se, so, inv = pl.pallas_call(
        first_kernel,
        out_shape=(
            weights(4), weights(2), f32(2), sends(2 * K + TB), sends(2 * K + TB), pltpu.SMEM((TL,), jnp.int32),
        ),
        in_specs=[HBM, SM, HBM, HBM, HBM],
        out_specs=(VM, VM, VM, VM, VM, SM),
        scratch_shapes=[
            pltpu.SMEM((TL,), jnp.int32),
            pltpu.SMEM((1, 2), jnp.int32),
            pltpu.VMEM((K, 4 * TB), F32),
            pltpu.SemaphoreType.DMA((8,)),
            pltpu.SemaphoreType.DMA((2,)),
        ],
        compiler_params=params(8),
        name="first",
    )(hbm(boundary), parity, hbm(tile_pair), hbm(modes), hbm(tiles))
    re, ro = exchange(se, so)
    inner_shapes = (f32(6), f32(4), f32(4), f32(2))
    w_in, j, mid, b, o = pl.pallas_call(
        load_kernel,
        out_shape=(weights(18),) + inner_shapes,
        in_specs=[SM, HBM, HBM, VM, VM],
        out_specs=(VM,) * 5,
        scratch_shapes=[
            pltpu.VMEM((K, ROWS), F32),
            pltpu.VMEM((K, ROWS), BF16),
            pltpu.VMEM((K, 6 * TB), BF16),
            pltpu.SemaphoreType.DMA((18,)),
            pltpu.SemaphoreType.DMA,
        ],
        compiler_params=params(12),
        cost_estimate=cost(40),
        name="load",
    )(inv, hbm(modes), hbm(tiles), pin(w_out), pin(w_edge))
    wn = None
    for k in range(2, DEG, 2):
        at_first = k == 2
        outs = pl.pallas_call(
            functools.partial(edge_kernel, at_first),
            out_shape=(f32(4), f32(2), sends(2 * K), sends(2 * K)) + ((weights(2),) if at_first else ()),
            in_specs=[SM] + [VM] * (7 if at_first else 8),
            out_specs=(VM,) * (5 if at_first else 4),
            compiler_params=params(8),
            name="edge",
        )(parity, re, ro, pin(z), pin(o), pin(b), pin(w_in), pin(w_out), *(() if at_first else (pin(wn),)))
        e, z, se, so = outs[:4]
        if at_first:
            wn = outs[4]
        re, ro = exchange(se, so)
        last = k == DEG - 2
        outs = pl.pallas_call(
            functools.partial(step_kernel, last),
            out_shape=inner_shapes + ((pltpu.VMEM((K, K), F32),) if last else ()),
            in_specs=[VM] * 6,
            out_specs=(VM,) * (5 if last else 4),
            scratch_shapes=[pltpu.VMEM((K, ROWS), BF16), pltpu.VMEM((K, 6 * TB), BF16)],
            compiler_params=params(8),
            cost_estimate=cost(40),
            name="step",
        )(pin(e), pin(mid), pin(j), pin(w_in), pin(w_out), pin(w_edge))
        j, mid, b, o = outs[:4]
    e, g = pl.pallas_call(
        final_kernel,
        out_shape=(f32(4), pltpu.VMEM((K // 2, 2 * K), F32)),
        in_specs=[SM] + [VM] * 9,
        out_specs=(VM, VM),
        compiler_params=params(8),
        name="final",
    )(parity, re, ro, pin(z), pin(o), pin(b), pin(w_in), pin(w_out), pin(wn), pin(outs[4]))
    for bits in (1, 3, 4, 12, 16, 32, 96):
        g = g + lax.ppermute(g, AXES, [(i, i ^ bits) for i in range(count)])
    return pl.pallas_call(
        functools.partial(whiten_kernel, 1.0 / (ROWS * count)),
        out_shape=jax.ShapeDtypeStruct((K, ROWS), F32),
        in_specs=[VM, VM, VM],
        out_specs=VM,
        compiler_params=params(16),
        name="whiten",
    )(g, pin(e), pin(mid))


def solution(mesh):
    placed = (
        P(None, AXES),
        P(AXES, None, None),
        P(AXES),
        P(AXES, None),
    )
    return jax.shard_map(
        local, mesh=mesh, in_specs=placed, out_specs=P(None, AXES), check_vma=False
    )
```

```python
import functools

import jax
import jax.numpy as jnp
from jax import lax
from jax.experimental import pallas as pl
from jax.experimental.pallas import tpu as pltpu
from jax.sharding import PartitionSpec as P

DEG = 8
center = 0.25
AXES = ("slab", "col")
K = 64
TB = 384
RT = 8
TL = 24
ROWS = RT * TB
F32 = jnp.float32
BF16 = jnp.bfloat16

VM = pl.BlockSpec(memory_space=pltpu.VMEM)
SM = pl.BlockSpec(memory_space=pltpu.SMEM)
HBM = pl.BlockSpec(memory_space=pltpu.HBM)


def pin(x):
    return pltpu.with_memory_space_constraint(x, pltpu.VMEM)


def hbm(x):
    return pltpu.with_memory_space_constraint(x, pltpu.HBM)


def params(mib):
    return pltpu.CompilerParams(vmem_limit_bytes=mib << 20)


def cost(tile_products):
    return pl.CostEstimate(flops=2 * K * TB * TB * tile_products, bytes_accessed=8 << 20, transcendentals=0)


def dot(a, b):
    return jnp.dot(a, b, preferred_element_type=F32)


def tile(i, n=1):
    return slice(i * TB, (i + n) * TB)


OUTER = [1, 3, 20, 22]
INNER = [3 * c + (r - c) + 1 for r in range(1, RT - 1) for c in (r - 1, r, r + 1)]


def inner(r, first=0, count=3):
    return tile(3 * (r - 1) + first, count)


def first_kernel(
    bound_ref, par_ref, pair_ref, modes_ref, tiles_ref,
    outer_ref, we_ref, z_ref, se_ref, so_ref, inv_ref,
    pair, bound, ym, sems, ssem,
):
    to_smem = pltpu.make_async_copy(pair_ref, pair, ssem.at[0])
    to_smem.start()
    bound_copy = pltpu.make_async_copy(bound_ref, bound, ssem.at[1])
    bound_copy.start()
    modes = [
        pltpu.make_async_copy(modes_ref.at[:, tile(0, 2)], ym.at[:, tile(0, 2)], sems.at[6]),
        pltpu.make_async_copy(modes_ref.at[:, tile(6, 2)], ym.at[:, tile(2, 2)], sems.at[7]),
    ]
    for c in modes:
        c.start()
    to_smem.wait()
    for t in range(TL):
        inv_ref[pair[t]] = t
    copies = [
        pltpu.make_async_copy(tiles_ref.at[inv_ref[p]], outer_ref.at[tile(i)], sems.at[i])
        for i, p in enumerate(OUTER)
    ] + [
        pltpu.make_async_copy(tiles_ref.at[inv_ref[p]], we_ref.at[tile(i)], sems.at[4 + i])
        for i, p in enumerate((0, TL - 1))
    ]
    for c in copies:
        c.start()
    bound_copy.wait()
    for c in modes + copies:
        c.wait()
    row = lax.broadcasted_iota(jnp.int32, (TB, TB), 0)
    zero = jnp.zeros((TB, TB), BF16)
    w_low = jnp.where(row < bound[0, 0], we_ref[tile(0)], zero)
    w_high = jnp.where(row >= TB - bound[0, 1], we_ref[tile(1)], zero)
    we_ref[tile(0)] = w_low
    we_ref[tile(1)] = w_high
    xs = ym[...].astype(BF16)
    z_low = dot(xs[:, tile(0, 2)], outer_ref[tile(0, 2)]) - center * ym[:, tile(0)]
    z_high = dot(xs[:, tile(2, 2)], outer_ref[tile(2, 2)]) - center * ym[:, tile(3)]
    z_ref[:, tile(0)] = z_low
    z_ref[:, tile(1)] = z_high
    even = par_ref[0] == 0
    send(even, xs[:, tile(0)], xs[:, tile(3)], z_low, z_high, se_ref, so_ref)
    se_ref[2 * K :] = jnp.where(even, w_high, w_low)
    so_ref[2 * K :] = jnp.where(even, w_low, w_high)


def send(even, x_low, x_high, z_low, z_high, se_ref, so_ref):
    z_low, z_high = z_low.astype(BF16), z_high.astype(BF16)
    se_ref[:K] = jnp.where(even, x_high, x_low)
    se_ref[K : 2 * K] = jnp.where(even, z_high, z_low)
    so_ref[:K] = jnp.where(even, x_low, x_high)
    so_ref[K : 2 * K] = jnp.where(even, z_low, z_high)


def interior(factor, previous, xs, ys, w_in, w_out, w_edge, j_ref, i_ref, b_ref, o_ref, xn):
    for r in range(1, RT - 1):
        acc = dot(xs[:, tile(r - 1, 3)], w_in[inner(r)]) - center * ys(r)
        nxt = acc if previous is None else factor * acc - previous(r)
        j_ref[:, tile(r - 1)] = nxt
        xn[:, tile(r - 1)] = nxt.astype(BF16)
    o_ref[:, tile(0)] = factor * dot(xs[:, tile(0)], w_edge[tile(0)])
    o_ref[:, tile(1)] = factor * dot(xs[:, tile(RT - 1)], w_edge[tile(1)])
    for r in range(2, RT - 2):
        acc = dot(xn[:, tile(r - 2, 3)], w_in[inner(r)]) - center * j_ref[:, tile(r - 1)]
        i_ref[:, tile(r - 2)] = 2.0 * acc - ys(r)
    b_ref[:, tile(0)] = 2.0 * dot(xn[:, tile(0)], w_out[tile(1)]) - ys(0)
    acc = dot(xn[:, tile(0, 2)], w_in[inner(1, 1, 2)]) - center * j_ref[:, tile(0)]
    b_ref[:, tile(1)] = 2.0 * acc - ys(1)
    acc = dot(xn[:, tile(4, 2)], w_in[inner(6, 0, 2)]) - center * j_ref[:, tile(5)]
    b_ref[:, tile(2)] = 2.0 * acc - ys(6)
    b_ref[:, tile(3)] = 2.0 * dot(xn[:, tile(5)], w_out[tile(2)]) - ys(7)


def load_kernel(
    inv_ref, modes_ref, tiles_ref, w_out, w_edge,
    w_in, j_ref, i_ref, b_ref, o_ref,
    y0, xs, xn, sems, msem,
):
    mcopy = pltpu.make_async_copy(modes_ref, y0, msem)
    mcopy.start()
    copies = [
        pltpu.make_async_copy(tiles_ref.at[inv_ref[p]], w_in.at[tile(i)], sems.at[i])
        for i, p in enumerate(INNER)
    ]
    for c in copies:
        c.start()
    mcopy.wait()
    for c in copies:
        c.wait()
    xs[...] = y0[...].astype(BF16)
    interior(1.0, None, xs, lambda r: y0[:, tile(r)], w_in, w_out, w_edge, j_ref, i_ref, b_ref, o_ref, xn)


def step_kernel(last, e_ref, m_ref, z_ref, w_in, w_out, w_edge, j_ref, i_ref, b_ref, o_ref, *rest):
    xs, xn = rest[-2:]
    xs[:, tile(0, 2)] = e_ref[:, tile(0, 2)].astype(BF16)
    xs[:, tile(2, 4)] = m_ref[...].astype(BF16)
    xs[:, tile(6, 2)] = e_ref[:, tile(2, 2)].astype(BF16)

    def ys(r):
        if r < 2:
            return e_ref[:, tile(r)]
        if r >= RT - 2:
            return e_ref[:, tile(r - 4)]
        return m_ref[:, tile(r - 2)]

    interior(
        2.0, lambda r: z_ref[:, tile(r - 1)], xs, ys, w_in, w_out, w_edge, j_ref, i_ref, b_ref, o_ref, xn
    )
    if last:
        rest[0][...] = gram(i_ref[...])


def gram(y):
    parts = jnp.concatenate(split(y), axis=0)
    p = lax.dot_general(parts, parts, (((1,), (1,)), ((), ())), preferred_element_type=F32)

    def block(a, b):
        return p[a * K : (a + 1) * K, b * K : (b + 1) * K]

    small = block(1, 1) + (block(0, 2) + block(2, 0))
    return block(0, 0) + ((block(0, 1) + block(1, 0)) + small)


def edges(factor, even, re_ref, ro_ref, z_ref, o_ref, b_ref, w_in, w_out, w_low, w_high):
    re, ro = re_ref[: 2 * K], ro_ref[: 2 * K]
    low, high = jnp.where(even, ro, re), jnp.where(even, re, ro)
    y_low = z_ref[:, tile(0)] + factor * dot(low[:K], w_low)
    y_high = z_ref[:, tile(1)] + factor * dot(high[:K], w_high)
    far_low = (low[K:].astype(F32) + o_ref[:, tile(0)]).astype(BF16)
    far_high = (high[K:].astype(F32) + o_ref[:, tile(1)]).astype(BF16)
    x_low, x_high = y_low.astype(BF16), y_high.astype(BF16)
    acc = dot(far_low, w_low) + dot(x_low, w_out[tile(0)]) - center * y_low
    e0 = b_ref[:, tile(0)] + 2.0 * acc
    acc = dot(far_high, w_high) + dot(x_high, w_out[tile(3)]) - center * y_high
    e3 = b_ref[:, tile(3)] + 2.0 * acc
    e1 = b_ref[:, tile(1)] + 2.0 * dot(x_low, w_in[inner(1, 0, 1)])
    e2 = b_ref[:, tile(2)] + 2.0 * dot(x_high, w_in[inner(6, 2, 1)])
    return y_low, y_high, (e0, e1, e2, e3)


def edge_kernel(
    at_first, par_ref, re_ref, ro_ref, z_ref, o_ref, b_ref, w_in, w_out, *rest
):
    even = par_ref[0] == 0
    if at_first:
        e_ref, zn_ref, se_ref, so_ref, wn_ref = rest
        we, wo = re_ref[2 * K :], ro_ref[2 * K :]
        w_low, w_high = jnp.where(even, wo, we), jnp.where(even, we, wo)
        wn_ref[tile(0)] = w_low
        wn_ref[tile(1)] = w_high
    else:
        wn_ref, e_ref, zn_ref, se_ref, so_ref = rest
    w_low, w_high = wn_ref[tile(0)], wn_ref[tile(1)]
    y_low, y_high, e = edges(
        1.0 if at_first else 2.0, even, re_ref, ro_ref, z_ref, o_ref, b_ref, w_in, w_out, w_low, w_high
    )
    for i in range(4):
        e_ref[:, tile(i)] = e[i]
    x = [v.astype(BF16) for v in e]
    z_low = 2.0 * (dot(x[0], w_out[tile(0)]) + dot(x[1], w_out[tile(1)]) - center * e[0]) - y_low
    z_high = 2.0 * (dot(x[2], w_out[tile(2)]) + dot(x[3], w_out[tile(3)]) - center * e[3]) - y_high
    zn_ref[:, tile(0)] = z_low
    zn_ref[:, tile(1)] = z_high
    send(even, x[0], x[3], z_low, z_high, se_ref, so_ref)


def final_kernel(par_ref, re_ref, ro_ref, z_ref, o_ref, b_ref, w_in, w_out, wn_ref, gi_ref, e_ref, g_ref):
    even = par_ref[0] == 0
    w_low, w_high = wn_ref[tile(0)], wn_ref[tile(1)]
    _, _, e = edges(2.0, even, re_ref, ro_ref, z_ref, o_ref, b_ref, w_in, w_out, w_low, w_high)
    for i in range(4):
        e_ref[:, tile(i)] = e[i]
    g = gi_ref[...] + gram(e_ref[...])
    g_ref[...] = jnp.concatenate([g[: K // 2], g[K // 2 :]], axis=1)


def split(x):
    high = x.astype(BF16)
    rest = x - high.astype(F32)
    mid = rest.astype(BF16)
    return high, mid, (rest - mid.astype(F32)).astype(BF16)


def inverse_factor(g):
    row = lax.broadcasted_iota(jnp.int32, (K, K), 0)
    col = lax.broadcasted_iota(jnp.int32, (K, K), 1)
    whole = jnp.concatenate([g, (row == col).astype(F32)], axis=1)
    count = K // 8
    shape = (8, 2 * K)
    blocks = [whole[8 * i : 8 * i + 8] for i in range(count)]
    sub = lax.broadcasted_iota(jnp.int32, shape, 0)
    scaled = []
    for b in range(count):
        rows = [jnp.broadcast_to(blocks[b][a : a + 1], shape) for a in range(8)]
        entry = {
            (a, c): jnp.broadcast_to(rows[a][:, 8 * b + c : 8 * b + c + 1], shape)
            for a in range(8)
            for c in range(8)
        }
        columns = {
            i: [jnp.broadcast_to(blocks[i][:, 8 * b + c : 8 * b + c + 1], shape) for c in range(8)]
            for i in range(b + 1, count)
        }
        pivots, inverses = rows[0], None
        for a in range(8):
            inverse = 1.0 / entry[a, a]
            inverses = inverse if a == 0 else jnp.where(sub == a, inverse, inverses)
            if a > 0:
                pivots = jnp.where(sub == a, rows[a], pivots)
            for r in range(a + 1, 8):
                m = entry[r, a] * inverse
                rows[r] = rows[r] - m * rows[a]
                for c in range(a + 1, 8):
                    entry[r, c] = entry[r, c] - m * entry[a, c]
            for i in columns:
                m = columns[i][a] * inverse
                for c in range(a + 1, 8):
                    columns[i][c] = columns[i][c] - m * entry[a, c]
                columns[i][a] = m
        for i in columns:
            update = columns[i][0] * rows[0]
            for a in range(1, 8):
                update = update + columns[i][a] * rows[a]
            blocks[i] = blocks[i] - update
        scaled.append(pivots * jnp.sqrt(inverses))
    return jnp.concatenate(scaled, axis=0)[:, K:]


def whiten_kernel(scale, g_ref, e_ref, i_ref, out_ref, buf, sems):
    g = g_ref[...] * scale
    high, mid, low = split(inverse_factor(jnp.concatenate([g[:, :K], g[:, K:]], axis=0)))
    left = jnp.concatenate([high, mid, high, low, mid, high], axis=1)
    copies = []
    for n in range(RT // 2):
        y = (e_ref[:, tile(0, 2)], i_ref[:, tile(0, 2)], i_ref[:, tile(2, 2)], e_ref[:, tile(2, 2)])[n]
        yh, ym, yl = split(y)
        right = jnp.concatenate([yh, yh, ym, yh, ym, yl], axis=0)
        buf[:, tile(2 * n, 2)] = dot(left, right)
        copy = pltpu.make_async_copy(buf.at[:, tile(2 * n, 2)], out_ref.at[:, tile(2 * n, 2)], sems.at[n])
        copy.start()
        copies.append(copy)
    for copy in copies:
        copy.wait()


def local(modes, tiles, tile_pair, boundary):
    count = lax.axis_size("slab") * lax.axis_size("col")
    parity = (lax.axis_index("col") & 1).astype(jnp.int32).reshape(1)
    pairs_even = [(i, i ^ 1) for i in range(count)]
    pairs_odd = [(i, (i + 1) % count if i % 2 else (i - 1) % count) for i in range(count)]

    def exchange(se, so):
        ro = lax.ppermute(so, AXES, pairs_odd)
        re = lax.ppermute(se, AXES, pairs_even)
        return re, ro

    def f32(tiles_wide):
        return pltpu.VMEM((K, tiles_wide * TB), F32)

    def weights(n):
        return pltpu.VMEM((n * TB, TB), BF16)

    def sends(rows):
        return pltpu.VMEM((rows, TB), BF16)

    w_out, w_edge, z, se, so, inv = pl.pallas_call(
        first_kernel,
        out_shape=(
            weights(4), weights(2), f32(2), sends(2 * K + TB), sends(2 * K + TB), pltpu.SMEM((TL,), jnp.int32),
        ),
        in_specs=[HBM, SM, HBM, HBM, HBM],
        out_specs=(VM, VM, VM, VM, VM, SM),
        scratch_shapes=[
            pltpu.SMEM((TL,), jnp.int32),
            pltpu.SMEM((1, 2), jnp.int32),
            pltpu.VMEM((K, 4 * TB), F32),
            pltpu.SemaphoreType.DMA((8,)),
            pltpu.SemaphoreType.DMA((2,)),
        ],
        compiler_params=params(8),
        name="first",
    )(hbm(boundary), parity, hbm(tile_pair), hbm(modes), hbm(tiles))
    re, ro = exchange(se, so)
    inner_shapes = (f32(6), f32(4), f32(4), f32(2))
    w_in, j, mid, b, o = pl.pallas_call(
        load_kernel,
        out_shape=(weights(18),) + inner_shapes,
        in_specs=[SM, HBM, HBM, VM, VM],
        out_specs=(VM,) * 5,
        scratch_shapes=[
            pltpu.VMEM((K, ROWS), F32),
            pltpu.VMEM((K, ROWS), BF16),
            pltpu.VMEM((K, 6 * TB), BF16),
            pltpu.SemaphoreType.DMA((18,)),
            pltpu.SemaphoreType.DMA,
        ],
        compiler_params=params(12),
        cost_estimate=cost(40),
        name="load",
    )(inv, hbm(modes), hbm(tiles), pin(w_out), pin(w_edge))
    wn = None
    for k in range(2, DEG, 2):
        at_first = k == 2
        outs = pl.pallas_call(
            functools.partial(edge_kernel, at_first),
            out_shape=(f32(4), f32(2), sends(2 * K), sends(2 * K)) + ((weights(2),) if at_first else ()),
            in_specs=[SM] + [VM] * (7 if at_first else 8),
            out_specs=(VM,) * (5 if at_first else 4),
            compiler_params=params(8),
            name="edge",
        )(parity, re, ro, pin(z), pin(o), pin(b), pin(w_in), pin(w_out), *(() if at_first else (pin(wn),)))
        e, z, se, so = outs[:4]
        if at_first:
            wn = outs[4]
        re, ro = exchange(se, so)
        last = k == DEG - 2
        outs = pl.pallas_call(
            functools.partial(step_kernel, last),
            out_shape=inner_shapes + ((pltpu.VMEM((K, K), F32),) if last else ()),
            in_specs=[VM] * 6,
            out_specs=(VM,) * (5 if last else 4),
            scratch_shapes=[pltpu.VMEM((K, ROWS), BF16), pltpu.VMEM((K, 6 * TB), BF16)],
            compiler_params=params(8),
            cost_estimate=cost(40),
            name="step",
        )(pin(e), pin(mid), pin(j), pin(w_in), pin(w_out), pin(w_edge))
        j, mid, b, o = outs[:4]
    e, g = pl.pallas_call(
        final_kernel,
        out_shape=(f32(4), pltpu.VMEM((K // 2, 2 * K), F32)),
        in_specs=[SM] + [VM] * 9,
        out_specs=(VM, VM),
        compiler_params=params(8),
        name="final",
    )(parity, re, ro, pin(z), pin(o), pin(b), pin(w_in), pin(w_out), pin(wn), pin(outs[4]))
    for group in ((16,), (1, 3, 2), (4, 12, 8), (32, 96, 64)):
        got = [lax.ppermute(g, AXES, [(i, i ^ bits) for i in range(count)]) for bits in group]
        for other in got:
            g = g + other
    return pl.pallas_call(
        functools.partial(whiten_kernel, 1.0 / (ROWS * count)),
        out_shape=jax.ShapeDtypeStruct((K, ROWS), F32),
        in_specs=[VM, VM, VM],
        out_specs=HBM,
        scratch_shapes=[pltpu.VMEM((K, ROWS), F32), pltpu.SemaphoreType.DMA((RT // 2,))],
        compiler_params=params(16),
        name="whiten",
    )(g, pin(e), pin(mid))


def solution(mesh):
    placed = (
        P(None, AXES),
        P(AXES, None, None),
        P(AXES),
        P(AXES, None),
    )
    return jax.shard_map(
        local, mesh=mesh, in_specs=placed, out_specs=P(None, AXES), check_vma=False
    )
```

```python
import functools

import jax
import jax.numpy as jnp
from jax import lax
from jax.experimental import pallas as pl
from jax.experimental.pallas import tpu as pltpu
from jax.sharding import PartitionSpec as P

DEG = 8
center = 0.25
AXES = ("slab", "col")
K = 64
TB = 384
RT = 8
TL = 24
ROWS = RT * TB
F32 = jnp.float32
BF16 = jnp.bfloat16

VM = pl.BlockSpec(memory_space=pltpu.VMEM)
SM = pl.BlockSpec(memory_space=pltpu.SMEM)
HBM = pl.BlockSpec(memory_space=pltpu.HBM)


def pin(x):
    return pltpu.with_memory_space_constraint(x, pltpu.VMEM)


def hbm(x):
    return pltpu.with_memory_space_constraint(x, pltpu.HBM)


def params(mib):
    return pltpu.CompilerParams(vmem_limit_bytes=mib << 20)


def cost(tile_products):
    return pl.CostEstimate(flops=2 * K * TB * TB * tile_products, bytes_accessed=8 << 20, transcendentals=0)


def dot(a, b):
    return jnp.dot(a, b, preferred_element_type=F32)


def tile(i, n=1):
    return slice(i * TB, (i + n) * TB)


OUTER = [1, 3, 20, 22]
INNER = [3 * c + (r - c) + 1 for r in range(1, RT - 1) for c in (r - 1, r, r + 1)]


def inner(r, first=0, count=3):
    return tile(3 * (r - 1) + first, count)


def first_kernel(
    bound_ref, par_ref, pair_ref, modes_ref, tiles_ref,
    outer_ref, we_ref, z_ref, se_ref, so_ref, inv_ref,
    pair, bound, ym, sems, ssem,
):
    to_smem = pltpu.make_async_copy(pair_ref, pair, ssem.at[0])
    to_smem.start()
    bound_copy = pltpu.make_async_copy(bound_ref, bound, ssem.at[1])
    bound_copy.start()
    modes = [
        pltpu.make_async_copy(modes_ref.at[:, tile(0, 2)], ym.at[:, tile(0, 2)], sems.at[6]),
        pltpu.make_async_copy(modes_ref.at[:, tile(6, 2)], ym.at[:, tile(2, 2)], sems.at[7]),
    ]
    for c in modes:
        c.start()
    to_smem.wait()
    for t in range(TL):
        inv_ref[pair[t]] = t
    copies = [
        pltpu.make_async_copy(tiles_ref.at[inv_ref[p]], outer_ref.at[tile(i)], sems.at[i])
        for i, p in enumerate(OUTER)
    ] + [
        pltpu.make_async_copy(tiles_ref.at[inv_ref[p]], we_ref.at[tile(i)], sems.at[4 + i])
        for i, p in enumerate((0, TL - 1))
    ]
    for c in copies:
        c.start()
    bound_copy.wait()
    for c in modes + copies:
        c.wait()
    row = lax.broadcasted_iota(jnp.int32, (TB, TB), 0)
    zero = jnp.zeros((TB, TB), BF16)
    w_low = jnp.where(row < bound[0, 0], we_ref[tile(0)], zero)
    w_high = jnp.where(row >= TB - bound[0, 1], we_ref[tile(1)], zero)
    we_ref[tile(0)] = w_low
    we_ref[tile(1)] = w_high
    xs = ym[...].astype(BF16)
    z_low = dot(xs[:, tile(0, 2)], outer_ref[tile(0, 2)]) - center * ym[:, tile(0)]
    z_high = dot(xs[:, tile(2, 2)], outer_ref[tile(2, 2)]) - center * ym[:, tile(3)]
    z_ref[:, tile(0)] = z_low
    z_ref[:, tile(1)] = z_high
    even = par_ref[0] == 0
    send(even, (xs[:, tile(0)], z_low), (xs[:, tile(3)], z_high), se_ref, so_ref)
    se_ref[2 * K :] = jnp.where(even, w_high, w_low)
    so_ref[2 * K :] = jnp.where(even, w_low, w_high)


def send(even, low, high, se_ref, so_ref):
    for i, (a, b) in enumerate(zip(low, high)):
        a, b = a.astype(BF16), b.astype(BF16)
        se_ref[i * K : (i + 1) * K] = jnp.where(even, b, a)
        so_ref[i * K : (i + 1) * K] = jnp.where(even, a, b)


def one_on(factor, now, before, xs, w_in, xn, keep):
    for r in range(1, RT - 1):
        acc = dot(xs[:, tile(r - 1, 3)], w_in[inner(r)]) - center * now(r)
        value = acc if before is None else factor * acc - before(r)
        keep(r, value)
        xn[:, tile(r - 1)] = value.astype(BF16)


def two_on(now, one, xn, w_in, w_out, b_ref, keep):
    for r in range(2, RT - 2):
        acc = dot(xn[:, tile(r - 2, 3)], w_in[inner(r)]) - center * one(r)
        keep(r, 2.0 * acc - now(r))
    b_ref[:, tile(0)] = 2.0 * dot(xn[:, tile(0)], w_out[tile(1)]) - now(0)
    acc = dot(xn[:, tile(0, 2)], w_in[inner(1, 1, 2)]) - center * one(1)
    b_ref[:, tile(1)] = 2.0 * acc - now(1)
    acc = dot(xn[:, tile(4, 2)], w_in[inner(6, 0, 2)]) - center * one(6)
    b_ref[:, tile(2)] = 2.0 * acc - now(6)
    b_ref[:, tile(3)] = 2.0 * dot(xn[:, tile(5)], w_out[tile(2)]) - now(7)


def overflow(factor, xs, w_edge, o_ref):
    o_ref[:, tile(0)] = factor * dot(xs[:, tile(0)], w_edge[tile(0)])
    o_ref[:, tile(1)] = factor * dot(xs[:, tile(RT - 1)], w_edge[tile(1)])


def load_kernel(
    par_ref, inv_ref, modes_ref, tiles_ref, w_out, w_edge,
    w_in, j_ref, m_ref, b_ref, o_ref, fe_ref, fo_ref,
    y0, xs, xn, sems, msem,
):
    mcopy = pltpu.make_async_copy(modes_ref, y0, msem)
    mcopy.start()
    copies = [
        pltpu.make_async_copy(tiles_ref.at[inv_ref[p]], w_in.at[tile(i)], sems.at[i])
        for i, p in enumerate(INNER)
    ]
    for c in copies:
        c.start()
    mcopy.wait()
    for c in copies:
        c.wait()
    xs[...] = y0[...].astype(BF16)
    even = par_ref[0] == 0
    w_low, w_high = w_out[tile(0)], w_out[tile(3)]
    fe_ref[...] = jnp.where(even, w_high, w_low)
    fo_ref[...] = jnp.where(even, w_low, w_high)

    def keep_one(r, value):
        j_ref[:, tile(r - 1)] = value

    def keep_two(r, value):
        m_ref[:, tile(r - 2)] = value

    def now(r):
        return y0[:, tile(r)]

    one_on(1.0, now, None, xs, w_in, xn, keep_one)
    overflow(1.0, xs, w_edge, o_ref)
    two_on(now, lambda r: j_ref[:, tile(r - 1)], xn, w_in, w_out, b_ref, keep_two)


def step_kernel(later, last, *refs):
    if later:
        e_ref, n_ref, p_ref, q_ref = refs[:4]
    else:
        e_ref, n_ref, p_ref = refs[:3]
    w_in, w_out, w_edge, m_ref, b_ref, o_ref, t_ref, c_ref, *rest = refs[4 if later else 3 :]
    xs, xn, xm, one_ref = rest[-4:]
    edge = 3 if later else 2

    def now(r):
        if r < edge:
            return e_ref[:, tile(r)]
        if r >= RT - edge:
            return e_ref[:, tile(r - RT + 2 * edge)]
        return n_ref[:, tile(r - edge)]

    def before(r):
        if not later:
            return p_ref[:, tile(r - 1)]
        if r in (1, 6):
            return p_ref[:, tile(0 if r == 1 else 1)]
        return q_ref[:, tile(r - 2)]

    def one(r):
        return one_ref[:, tile(r - 1)]

    def keep_one(r, value):
        one_ref[:, tile(r - 1)] = value

    def keep_two(r, value):
        m_ref[:, tile(r - 2)] = value
        xm[:, tile(r - 2)] = value.astype(BF16)

    for r in range(RT):
        xs[:, tile(r)] = now(r).astype(BF16)
    one_on(2.0, now, before, xs, w_in, xn, keep_one)
    overflow(2.0, xs, w_edge, o_ref)
    two_on(now, one, xn, w_in, w_out, b_ref, keep_two)
    for r in (3, 4):
        acc = dot(xm[:, tile(r - 3, 3)], w_in[inner(r)]) - center * m_ref[:, tile(r - 2)]
        t_ref[:, tile(r - 3)] = 2.0 * acc - one(r)
    c_ref[:, tile(0)] = 2.0 * dot(xm[:, tile(0)], w_in[inner(1, 2, 1)]) - one(1)
    acc = dot(xm[:, tile(0, 2)], w_in[inner(2, 1, 2)]) - center * m_ref[:, tile(0)]
    c_ref[:, tile(1)] = 2.0 * acc - one(2)
    acc = dot(xm[:, tile(2, 2)], w_in[inner(5, 0, 2)]) - center * m_ref[:, tile(3)]
    c_ref[:, tile(2)] = 2.0 * acc - one(5)
    c_ref[:, tile(3)] = 2.0 * dot(xm[:, tile(3)], w_in[inner(6, 0, 1)]) - one(6)
    if last:
        rest[0][...] = gram(t_ref[...])


def gram(y):
    parts = jnp.concatenate(split(y), axis=0)
    p = lax.dot_general(parts, parts, (((1,), (1,)), ((), ())), preferred_element_type=F32)

    def block(a, b):
        return p[a * K : (a + 1) * K, b * K : (b + 1) * K]

    small = block(1, 1) + (block(0, 2) + block(2, 0))
    return block(0, 0) + ((block(0, 1) + block(1, 0)) + small)


def bf(x):
    return x.astype(BF16)


def side_weights(side, w_in, w_out):
    if side == 0:
        rows = {(0, 0): w_out[tile(0)], (1, 0): w_out[tile(1)]}
        near, far = (0, 1, 2), (0, 1, 2)
    else:
        rows = {(0, 0): w_out[tile(3)], (1, 0): w_out[tile(2)]}
        near, far = (2, 1, 0), (2, 1, 0)
    first, second = (1, 2) if side == 0 else (6, 5)
    for source in range(3):
        rows[source, 1] = w_in[inner(first, near[source], 1)]
    rows[1, 2] = w_in[inner(second, far[0], 1)]
    return rows


def chosen(even, re, ro):
    return jnp.where(even, ro, re), jnp.where(even, re, ro)


def prepare(ws, ys, x2s, before):
    both = range(2)
    x = [[bf(y) for y in ys[i][:2]] for i in both]
    next1 = [dot(x[i][1], ws[i][1, 1]) + dot(x2s[i], ws[i][2, 1]) for i in both]
    next1 = [next1[i] + dot(x[i][0], ws[i][0, 1]) for i in both]
    next1 = [bf(2.0 * (next1[i] - center * ys[i][1]) - before[i][1]) for i in both]
    z = [dot(x[i][0], ws[i][0, 0]) + dot(x[i][1], ws[i][1, 0]) for i in both]
    s = [2.0 * dot(next1[i], ws[i][1, 0]) - ys[i][0] for i in both]
    z = [2.0 * (z[i] - center * ys[i][0]) - before[i][0] for i in both]
    return z, [(x[i][0], z[i], s[i]) for i in both]


def edge2_kernel(
    par_ref, re_ref, ro_ref, z_ref, o_ref, b_ref, w_in, w_out, m_ref, j_ref,
    e_ref, zn_ref, se_ref, so_ref, wn_ref,
):
    even = par_ref[0] == 0
    got = chosen(even, re_ref[: 2 * K], ro_ref[: 2 * K])
    for side, w in enumerate(chosen(even, re_ref[2 * K :], ro_ref[2 * K :])):
        wn_ref[tile(side)] = w
    both = range(2)
    w = [side_weights(i, w_in, w_out) for i in both]
    wn = [wn_ref[tile(i)] for i in both]
    outer, second = (0, 3), (1, 2)
    far = [bf(got[i][K:].astype(F32) + o_ref[:, tile(i)]) for i in both]
    share = [dot(jnp.concatenate([got[i][:K], far[i]], axis=0), wn[i]) for i in both]
    y0_1 = [z_ref[:, tile(i)] + share[i][:K] for i in both]
    x0_1 = [bf(y) for y in y0_1]
    y1 = [b_ref[:, tile(second[i])] + 2.0 * dot(x0_1[i], w[i][0, 1]) for i in both]
    y0 = [dot(x0_1[i], w[i][0, 0]) + share[i][K:] for i in both]
    y0 = [b_ref[:, tile(outer[i])] + 2.0 * (y0[i] - center * y0_1[i]) for i in both]
    for i in both:
        e_ref[:, tile(outer[i])] = y0[i]
        e_ref[:, tile(second[i])] = y1[i]
    x2 = [bf(m_ref[:, tile(3 * i)]) for i in both]
    before = [(y0_1[i], j_ref[:, tile(5 * i)]) for i in both]
    z, parts = prepare(w, [(y0[i], y1[i]) for i in both], x2, before)
    for i in both:
        zn_ref[:, tile(i)] = z[i]
    send(even, parts[0], parts[1], se_ref, so_ref)


def three_on(got, w, wn, wf, we, z_ref, o_ref, b_ref, c_ref):
    both = range(2)
    outer, second = (0, 3), (1, 2)
    far1 = [got[i][K : 2 * K].astype(F32) + o_ref[:, tile(i)] for i in both]
    xf = [bf(f) for f in far1]
    share = [dot(jnp.concatenate([got[i][:K], xf[i]], axis=0), wn[i]) for i in both]
    y0_1 = [z_ref[:, tile(i)] + 2.0 * share[i][:K] for i in both]
    x0 = [bf(y) for y in y0_1]
    far2 = [dot(xf[i], wf[i]) for i in both]
    y1_2 = [b_ref[:, tile(second[i])] + 2.0 * dot(x0[i], w[i][0, 1]) for i in both]
    y0_2 = [dot(x0[i], w[i][0, 0]) + share[i][K:] for i in both]
    far2 = [far2[i] + dot(x0[i], we[i]) for i in both]
    y0_2 = [b_ref[:, tile(outer[i])] + 2.0 * (y0_2[i] - center * y0_1[i]) for i in both]
    far2 = [got[i][2 * K :].astype(F32) + 2.0 * (far2[i] - center * far1[i]) for i in both]
    x1, x0, xf = [bf(y) for y in y1_2], [bf(y) for y in y0_2], [bf(f) for f in far2]
    y2_3 = [c_ref[:, tile(second[i])] + 2.0 * dot(x1[i], w[i][1, 2]) for i in both]
    y1_3 = [dot(x1[i], w[i][1, 1]) + dot(x0[i], w[i][0, 1]) for i in both]
    y0_3 = [dot(x1[i], w[i][1, 0]) + dot(x0[i], w[i][0, 0]) + dot(xf[i], wn[i]) for i in both]
    y1_3 = [c_ref[:, tile(outer[i])] + 2.0 * (y1_3[i] - center * y1_2[i]) for i in both]
    y0_3 = [2.0 * (y0_3[i] - center * y0_2[i]) - y0_1[i] for i in both]
    return list(zip(y0_2, y1_2)), list(zip(y0_3, y1_3, y2_3))


def edge3_kernel(
    last, par_ref, re_ref, ro_ref, z_ref, o_ref, b_ref, c_ref, w_in, w_out, wn_ref, w_edge, fe_ref, fo_ref, *rest
):
    even = par_ref[0] == 0
    got = chosen(even, re_ref[...], ro_ref[...])
    far = chosen(even, fe_ref[...], fo_ref[...])
    e_ref = rest[1] if last else rest[0]
    both = range(2)
    w = [side_weights(i, w_in, w_out) for i in both]
    wn, we = [wn_ref[tile(i)] for i in both], [w_edge[tile(i)] for i in both]
    two, three = three_on(got, w, wn, far, we, z_ref, o_ref, b_ref, c_ref)
    for i in both:
        for n in range(3):
            e_ref[:, tile(5 - n if i else n)] = three[i][n]
    if not last:
        _, p_ref, zn_ref, _, _ = rest
        z, parts = prepare(w, three, [bf(y[2]) for y in three], two)
        for i in both:
            p_ref[:, tile(i)] = two[i][1]
            zn_ref[:, tile(i)] = z[i]
    if last:
        g = rest[0][...] + gram(e_ref[...])
        rest[2][...] = jnp.concatenate([g[: K // 2], g[K // 2 :]], axis=1)
    else:
        send(even, parts[0], parts[1], rest[3], rest[4])


def split(x):
    high = x.astype(BF16)
    rest = x - high.astype(F32)
    mid = rest.astype(BF16)
    return high, mid, (rest - mid.astype(F32)).astype(BF16)


def inverse_factor(g):
    row = lax.broadcasted_iota(jnp.int32, (K, K), 0)
    col = lax.broadcasted_iota(jnp.int32, (K, K), 1)
    whole = jnp.concatenate([g, (row == col).astype(F32)], axis=1)
    count = K // 8
    shape = (8, 2 * K)
    blocks = [whole[8 * i : 8 * i + 8] for i in range(count)]
    sub = lax.broadcasted_iota(jnp.int32, shape, 0)
    scaled = []
    for b in range(count):
        rows = [jnp.broadcast_to(blocks[b][a : a + 1], shape) for a in range(8)]
        entry = {
            (a, c): jnp.broadcast_to(rows[a][:, 8 * b + c : 8 * b + c + 1], shape)
            for a in range(8)
            for c in range(8)
        }
        columns = {
            i: [jnp.broadcast_to(blocks[i][:, 8 * b + c : 8 * b + c + 1], shape) for c in range(8)]
            for i in range(b + 1, count)
        }
        pivots, inverses = rows[0], None
        for a in range(8):
            inverse = 1.0 / entry[a, a]
            inverses = inverse if a == 0 else jnp.where(sub == a, inverse, inverses)
            if a > 0:
                pivots = jnp.where(sub == a, rows[a], pivots)
            for r in range(a + 1, 8):
                m = entry[r, a] * inverse
                rows[r] = rows[r] - m * rows[a]
                for c in range(a + 1, 8):
                    entry[r, c] = entry[r, c] - m * entry[a, c]
            for i in columns:
                m = columns[i][a] * inverse
                for c in range(a + 1, 8):
                    columns[i][c] = columns[i][c] - m * entry[a, c]
                columns[i][a] = m
        for i in columns:
            update = columns[i][0] * rows[0]
            for a in range(1, 8):
                update = update + columns[i][a] * rows[a]
            blocks[i] = blocks[i] - update
        scaled.append(pivots * jnp.sqrt(inverses))
    return jnp.concatenate(scaled, axis=0)[:, K:]


def whiten_kernel(scale, g_ref, e_ref, i_ref, out_ref, buf, sems):
    g = g_ref[...] * scale
    high, mid, low = split(inverse_factor(jnp.concatenate([g[:, :K], g[:, K:]], axis=0)))
    left = jnp.concatenate([high, mid, high, low, mid, high], axis=1)
    copies = []
    for n, (at, y) in enumerate(
        ((tile(0, 3), e_ref[:, tile(0, 3)]), (tile(3, 2), i_ref[...]), (tile(5, 3), e_ref[:, tile(3, 3)]))
    ):
        yh, ym, yl = split(y)
        right = jnp.concatenate([yh, yh, ym, yh, ym, yl], axis=0)
        buf[:, at] = dot(left, right)
        copy = pltpu.make_async_copy(buf.at[:, at], out_ref.at[:, at], sems.at[n])
        copy.start()
        copies.append(copy)
    for copy in copies:
        copy.wait()


def local(modes, tiles, tile_pair, boundary):
    count = lax.axis_size("slab") * lax.axis_size("col")
    parity = (lax.axis_index("col") & 1).astype(jnp.int32).reshape(1)
    pairs_even = [(i, i ^ 1) for i in range(count)]
    pairs_odd = [(i, (i + 1) % count if i % 2 else (i - 1) % count) for i in range(count)]

    def exchange(se, so):
        ro = lax.ppermute(so, AXES, pairs_odd)
        re = lax.ppermute(se, AXES, pairs_even)
        return re, ro

    def f32(tiles_wide):
        return pltpu.VMEM((K, tiles_wide * TB), F32)

    def weights(n):
        return pltpu.VMEM((n * TB, TB), BF16)

    def sends(rows):
        return pltpu.VMEM((rows, TB), BF16)

    w_out, w_edge, z, se, so, inv = pl.pallas_call(
        first_kernel,
        out_shape=(
            weights(4), weights(2), f32(2), sends(2 * K + TB), sends(2 * K + TB), pltpu.SMEM((TL,), jnp.int32),
        ),
        in_specs=[HBM, SM, HBM, HBM, HBM],
        out_specs=(VM, VM, VM, VM, VM, SM),
        scratch_shapes=[
            pltpu.SMEM((TL,), jnp.int32),
            pltpu.SMEM((1, 2), jnp.int32),
            pltpu.VMEM((K, 4 * TB), F32),
            pltpu.SemaphoreType.DMA((8,)),
            pltpu.SemaphoreType.DMA((2,)),
        ],
        compiler_params=params(8),
        name="first",
    )(hbm(boundary), parity, hbm(tile_pair), hbm(modes), hbm(tiles))
    re, ro = exchange(se, so)
    w_in, j, m, b, o, fe, fo = pl.pallas_call(
        load_kernel,
        out_shape=(weights(18), f32(6), f32(4), f32(4), f32(2), weights(1), weights(1)),
        in_specs=[SM, SM, HBM, HBM, VM, VM],
        out_specs=(VM,) * 7,
        scratch_shapes=[
            pltpu.VMEM((K, ROWS), F32),
            pltpu.VMEM((K, ROWS), BF16),
            pltpu.VMEM((K, 6 * TB), BF16),
            pltpu.SemaphoreType.DMA((18,)),
            pltpu.SemaphoreType.DMA,
        ],
        compiler_params=params(12),
        cost_estimate=cost(40),
        name="load",
    )(parity, inv, hbm(modes), hbm(tiles), pin(w_out), pin(w_edge))
    fe, fo = exchange(fe, fo)
    e, z, se, so, wn = pl.pallas_call(
        edge2_kernel,
        out_shape=(f32(4), f32(2), sends(3 * K), sends(3 * K), weights(2)),
        in_specs=[SM] + [VM] * 9,
        out_specs=(VM,) * 5,
        compiler_params=params(8),
        name="edge2",
    )(parity, re, ro, pin(z), pin(o), pin(b), pin(w_in), pin(w_out), pin(m), pin(j))
    state = (e, m, j)
    for later in (False, True):
        re, ro = exchange(se, so)
        outs = pl.pallas_call(
            functools.partial(step_kernel, later, later),
            out_shape=(f32(4), f32(4), f32(2), f32(2), f32(4)) + ((pltpu.VMEM((K, K), F32),) if later else ()),
            in_specs=[VM] * (len(state) + 3),
            out_specs=(VM,) * (6 if later else 5),
            scratch_shapes=[
                pltpu.VMEM((K, ROWS), BF16),
                pltpu.VMEM((K, 6 * TB), BF16),
                pltpu.VMEM((K, 4 * TB), BF16),
                pltpu.VMEM((K, 6 * TB), F32),
            ],
            compiler_params=params(10),
            cost_estimate=cost(52),
            name="step",
        )(*(pin(x) for x in state), pin(w_in), pin(w_out), pin(w_edge))
        m, b, o, t, c = outs[:5]
        shared = (
            parity, re, ro, pin(z), pin(o), pin(b), pin(c), pin(w_in), pin(w_out), pin(wn), pin(w_edge), fe, fo
        )
        if not later:
            e, p, z, se, so = pl.pallas_call(
                functools.partial(edge3_kernel, False),
                out_shape=(f32(6), f32(2), f32(2), sends(3 * K), sends(3 * K)),
                in_specs=[SM] + [VM] * 12,
                out_specs=(VM,) * 5,
                compiler_params=params(8),
                name="edge3",
            )(*shared)
            state = (e, t, p, m)
    e, g = pl.pallas_call(
        functools.partial(edge3_kernel, True),
        out_shape=(f32(6), pltpu.VMEM((K // 2, 2 * K), F32)),
        in_specs=[SM] + [VM] * 13,
        out_specs=(VM, VM),
        compiler_params=params(8),
        name="final",
    )(*shared, pin(outs[5]))
    for group in ((16,), (1, 3, 2), (4, 12, 8), (32, 96, 64)):
        got = [lax.ppermute(g, AXES, [(i, i ^ bits) for i in range(count)]) for bits in group]
        for other in got:
            g = g + other
    return pl.pallas_call(
        functools.partial(whiten_kernel, 1.0 / (ROWS * count)),
        out_shape=jax.ShapeDtypeStruct((K, ROWS), F32),
        in_specs=[VM, VM, VM],
        out_specs=HBM,
        scratch_shapes=[pltpu.VMEM((K, ROWS), F32), pltpu.SemaphoreType.DMA((3,))],
        compiler_params=params(16),
        name="whiten",
    )(g, pin(e), pin(t))


def solution(mesh):
    placed = (
        P(None, AXES),
        P(AXES, None, None),
        P(AXES),
        P(AXES, None),
    )
    return jax.shard_map(
        local, mesh=mesh, in_specs=placed, out_specs=P(None, AXES), check_vma=False
    )
```

```python
import functools

import jax
import jax.numpy as jnp
from jax import lax
from jax.experimental import pallas as pl
from jax.experimental.pallas import tpu as pltpu
from jax.sharding import PartitionSpec as P

DEG = 8
center = 0.25
AXES = ("slab", "col")
K = 64
TB = 384
RT = 8
TL = 24
ROWS = RT * TB
F32 = jnp.float32
BF16 = jnp.bfloat16

VM = pl.BlockSpec(memory_space=pltpu.VMEM)
SM = pl.BlockSpec(memory_space=pltpu.SMEM)
HBM = pl.BlockSpec(memory_space=pltpu.HBM)


def pin(x):
    return pltpu.with_memory_space_constraint(x, pltpu.VMEM)


def hbm(x):
    return pltpu.with_memory_space_constraint(x, pltpu.HBM)


def params(mib):
    return pltpu.CompilerParams(vmem_limit_bytes=mib << 20)


def cost(tile_products):
    return pl.CostEstimate(flops=2 * K * TB * TB * tile_products, bytes_accessed=8 << 20, transcendentals=0)


def dot(a, b):
    return jnp.dot(a, b, preferred_element_type=F32)


def is_even():
    return lax.rem(lax.axis_index("col"), 2) == 0


def tile(i, n=1):
    return slice(i * TB, (i + n) * TB)


OUTER = [1, 3, 20, 22]
INNER = [3 * c + (r - c) + 1 for r in range(1, RT - 1) for c in (r - 1, r, r + 1)]


def inner(r, first=0, count=3):
    return tile(3 * (r - 1) + first, count)


def first_kernel(
    bound_ref, pair_ref, modes_ref, tiles_ref,
    outer_ref, we_ref, z_ref, se_ref, so_ref, inv_ref,
    pair, bound, ym, sems, ssem,
):
    to_smem = pltpu.make_async_copy(pair_ref, pair, ssem.at[0])
    to_smem.start()
    bound_copy = pltpu.make_async_copy(bound_ref, bound, ssem.at[1])
    bound_copy.start()
    modes = [
        pltpu.make_async_copy(modes_ref.at[:, tile(0, 2)], ym.at[:, tile(0, 2)], sems.at[6]),
        pltpu.make_async_copy(modes_ref.at[:, tile(6, 2)], ym.at[:, tile(2, 2)], sems.at[7]),
    ]
    for c in modes:
        c.start()
    to_smem.wait()
    for t in range(TL):
        inv_ref[pair[t]] = t
    edge_copies = [
        pltpu.make_async_copy(tiles_ref.at[inv_ref[p]], we_ref.at[tile(i)], sems.at[4 + i])
        for i, p in enumerate((0, TL - 1))
    ]
    outer_copies = [
        pltpu.make_async_copy(tiles_ref.at[inv_ref[p]], outer_ref.at[tile(i)], sems.at[i])
        for i, p in enumerate(OUTER)
    ]
    for c in edge_copies + outer_copies:
        c.start()
    for c in modes:
        c.wait()
    xs = ym[...].astype(BF16)
    bound_copy.wait()
    for c in edge_copies:
        c.wait()
    row = lax.broadcasted_iota(jnp.int32, (TB, TB), 0)
    zero = jnp.zeros((TB, TB), BF16)
    w_low = jnp.where(row < bound[0, 0], we_ref[tile(0)], zero)
    w_high = jnp.where(row >= TB - bound[0, 1], we_ref[tile(1)], zero)
    we_ref[tile(0)] = w_low
    we_ref[tile(1)] = w_high
    even = is_even()
    se_ref[2 * K :] = jnp.where(even, w_high, w_low)
    so_ref[2 * K :] = jnp.where(even, w_low, w_high)
    for c in outer_copies:
        c.wait()
    z_low = dot(xs[:, tile(0, 2)], outer_ref[tile(0, 2)]) - center * ym[:, tile(0)]
    z_high = dot(xs[:, tile(2, 2)], outer_ref[tile(2, 2)]) - center * ym[:, tile(3)]
    z_ref[:, tile(0)] = z_low
    z_ref[:, tile(1)] = z_high
    send(even, (xs[:, tile(0)], z_low), (xs[:, tile(3)], z_high), se_ref, so_ref)


def send(even, low, high, se_ref, so_ref):
    for i, (a, b) in enumerate(zip(low, high)):
        a, b = a.astype(BF16), b.astype(BF16)
        se_ref[i * K : (i + 1) * K] = jnp.where(even, b, a)
        so_ref[i * K : (i + 1) * K] = jnp.where(even, a, b)


def one_on(factor, now, before, xs, w_in, xn, keep):
    for r in range(1, RT - 1):
        acc = dot(xs[:, tile(r - 1, 3)], w_in[inner(r)]) - center * now(r)
        value = acc if before is None else factor * acc - before(r)
        keep(r, value)
        xn[:, tile(r - 1)] = value.astype(BF16)


def two_on(now, one, xn, w_in, w_out, b_ref, keep):
    for r in range(2, RT - 2):
        acc = dot(xn[:, tile(r - 2, 3)], w_in[inner(r)]) - center * one(r)
        keep(r, 2.0 * acc - now(r))
    b_ref[:, tile(0)] = 2.0 * dot(xn[:, tile(0)], w_out[tile(1)]) - now(0)
    acc = dot(xn[:, tile(0, 2)], w_in[inner(1, 1, 2)]) - center * one(1)
    b_ref[:, tile(1)] = 2.0 * acc - now(1)
    acc = dot(xn[:, tile(4, 2)], w_in[inner(6, 0, 2)]) - center * one(6)
    b_ref[:, tile(2)] = 2.0 * acc - now(6)
    b_ref[:, tile(3)] = 2.0 * dot(xn[:, tile(5)], w_out[tile(2)]) - now(7)


def overflow(factor, xs, w_edge, o_ref):
    o_ref[:, tile(0)] = factor * dot(xs[:, tile(0)], w_edge[tile(0)])
    o_ref[:, tile(1)] = factor * dot(xs[:, tile(RT - 1)], w_edge[tile(1)])


def load_kernel(
    inv_ref, modes_ref, tiles_ref, w_out, w_edge,
    w_in, j_ref, m_ref, b_ref, o_ref, fe_ref, fo_ref,
    y0, xs, xn, sems, msem,
):
    mcopy = pltpu.make_async_copy(modes_ref, y0, msem)
    mcopy.start()
    copies = [
        pltpu.make_async_copy(tiles_ref.at[inv_ref[p]], w_in.at[tile(i)], sems.at[i])
        for i, p in enumerate(INNER)
    ]
    for c in copies:
        c.start()
    mcopy.wait()
    for c in copies:
        c.wait()
    xs[...] = y0[...].astype(BF16)
    even = is_even()
    w_low, w_high = w_out[tile(0)], w_out[tile(3)]
    fe_ref[...] = jnp.where(even, w_high, w_low)
    fo_ref[...] = jnp.where(even, w_low, w_high)

    def keep_one(r, value):
        j_ref[:, tile(r - 1)] = value

    def keep_two(r, value):
        m_ref[:, tile(r - 2)] = value

    def now(r):
        return y0[:, tile(r)]

    one_on(1.0, now, None, xs, w_in, xn, keep_one)
    overflow(1.0, xs, w_edge, o_ref)
    two_on(now, lambda r: j_ref[:, tile(r - 1)], xn, w_in, w_out, b_ref, keep_two)


def step_kernel(later, last, *refs):
    if later:
        e_ref, n_ref, p_ref, q_ref = refs[:4]
    else:
        e_ref, n_ref, p_ref = refs[:3]
    w_in, w_out, w_edge, m_ref, b_ref, o_ref, t_ref, c_ref, *rest = refs[4 if later else 3 :]
    xs, xn, xm, one_ref = rest[-4:]
    edge = 3 if later else 2

    def now(r):
        if r < edge:
            return e_ref[:, tile(r)]
        if r >= RT - edge:
            return e_ref[:, tile(r - RT + 2 * edge)]
        return n_ref[:, tile(r - edge)]

    def before(r):
        if not later:
            return p_ref[:, tile(r - 1)]
        if r in (1, 6):
            return p_ref[:, tile(0 if r == 1 else 1)]
        return q_ref[:, tile(r - 2)]

    def one(r):
        return one_ref[:, tile(r - 1)]

    def keep_one(r, value):
        one_ref[:, tile(r - 1)] = value

    def keep_two(r, value):
        m_ref[:, tile(r - 2)] = value
        xm[:, tile(r - 2)] = value.astype(BF16)

    for r in range(RT):
        xs[:, tile(r)] = now(r).astype(BF16)
    one_on(2.0, now, before, xs, w_in, xn, keep_one)
    overflow(2.0, xs, w_edge, o_ref)
    two_on(now, one, xn, w_in, w_out, b_ref, keep_two)
    for r in (3, 4):
        acc = dot(xm[:, tile(r - 3, 3)], w_in[inner(r)]) - center * m_ref[:, tile(r - 2)]
        t_ref[:, tile(r - 3)] = 2.0 * acc - one(r)
    c_ref[:, tile(0)] = 2.0 * dot(xm[:, tile(0)], w_in[inner(1, 2, 1)]) - one(1)
    acc = dot(xm[:, tile(0, 2)], w_in[inner(2, 1, 2)]) - center * m_ref[:, tile(0)]
    c_ref[:, tile(1)] = 2.0 * acc - one(2)
    acc = dot(xm[:, tile(2, 2)], w_in[inner(5, 0, 2)]) - center * m_ref[:, tile(3)]
    c_ref[:, tile(2)] = 2.0 * acc - one(5)
    c_ref[:, tile(3)] = 2.0 * dot(xm[:, tile(3)], w_in[inner(6, 0, 1)]) - one(6)
    if last:
        rest[0][...] = gram(t_ref[...])


def gram(y):
    parts = jnp.concatenate(split(y), axis=0)
    p = lax.dot_general(parts, parts, (((1,), (1,)), ((), ())), preferred_element_type=F32)

    def block(a, b):
        return p[a * K : (a + 1) * K, b * K : (b + 1) * K]

    small = block(1, 1) + (block(0, 2) + block(2, 0))
    return block(0, 0) + ((block(0, 1) + block(1, 0)) + small)


def bf(x):
    return x.astype(BF16)


def side_weights(side, w_in, w_out):
    if side == 0:
        rows = {(0, 0): w_out[tile(0)], (1, 0): w_out[tile(1)]}
        near, far = (0, 1, 2), (0, 1, 2)
    else:
        rows = {(0, 0): w_out[tile(3)], (1, 0): w_out[tile(2)]}
        near, far = (2, 1, 0), (2, 1, 0)
    first, second = (1, 2) if side == 0 else (6, 5)
    for source in range(3):
        rows[source, 1] = w_in[inner(first, near[source], 1)]
    rows[1, 2] = w_in[inner(second, far[0], 1)]
    return rows


def chosen(even, re, ro):
    return jnp.where(even, ro, re), jnp.where(even, re, ro)


def prepare(ws, ys, x2s, before):
    both = range(2)
    x = [[bf(y) for y in ys[i][:2]] for i in both]
    next1 = [dot(x[i][1], ws[i][1, 1]) + dot(x2s[i], ws[i][2, 1]) for i in both]
    next1 = [next1[i] + dot(x[i][0], ws[i][0, 1]) for i in both]
    next1 = [bf(2.0 * (next1[i] - center * ys[i][1]) - before[i][1]) for i in both]
    z = [dot(x[i][0], ws[i][0, 0]) + dot(x[i][1], ws[i][1, 0]) for i in both]
    s = [2.0 * dot(next1[i], ws[i][1, 0]) - ys[i][0] for i in both]
    z = [2.0 * (z[i] - center * ys[i][0]) - before[i][0] for i in both]
    return z, [(x[i][0], z[i], s[i]) for i in both]


def edge2_kernel(
    re_ref, ro_ref, z_ref, o_ref, b_ref, w_in, w_out, m_ref, j_ref,
    e_ref, zn_ref, se_ref, so_ref, wn_ref,
):
    even = is_even()
    got = chosen(even, re_ref[: 2 * K], ro_ref[: 2 * K])
    for side, w in enumerate(chosen(even, re_ref[2 * K :], ro_ref[2 * K :])):
        wn_ref[tile(side)] = w
    both = range(2)
    w = [side_weights(i, w_in, w_out) for i in both]
    wn = [wn_ref[tile(i)] for i in both]
    outer, second = (0, 3), (1, 2)
    far = [bf(got[i][K:].astype(F32) + o_ref[:, tile(i)]) for i in both]
    share = [dot(jnp.concatenate([got[i][:K], far[i]], axis=0), wn[i]) for i in both]
    y0_1 = [z_ref[:, tile(i)] + share[i][:K] for i in both]
    x0_1 = [bf(y) for y in y0_1]
    y1 = [b_ref[:, tile(second[i])] + 2.0 * dot(x0_1[i], w[i][0, 1]) for i in both]
    y0 = [dot(x0_1[i], w[i][0, 0]) + share[i][K:] for i in both]
    y0 = [b_ref[:, tile(outer[i])] + 2.0 * (y0[i] - center * y0_1[i]) for i in both]
    for i in both:
        e_ref[:, tile(outer[i])] = y0[i]
        e_ref[:, tile(second[i])] = y1[i]
    x2 = [bf(m_ref[:, tile(3 * i)]) for i in both]
    before = [(y0_1[i], j_ref[:, tile(5 * i)]) for i in both]
    z, parts = prepare(w, [(y0[i], y1[i]) for i in both], x2, before)
    for i in both:
        zn_ref[:, tile(i)] = z[i]
    send(even, parts[0], parts[1], se_ref, so_ref)


def three_on(got, w, wn, wf, we, z_ref, o_ref, b_ref, c_ref):
    both = range(2)
    outer, second = (0, 3), (1, 2)
    far1 = [got[i][K : 2 * K].astype(F32) + o_ref[:, tile(i)] for i in both]
    xf = [bf(f) for f in far1]
    share = [dot(jnp.concatenate([got[i][:K], xf[i]], axis=0), wn[i]) for i in both]
    y0_1 = [z_ref[:, tile(i)] + 2.0 * share[i][:K] for i in both]
    x0 = [bf(y) for y in y0_1]
    far2 = [dot(xf[i], wf[i]) for i in both]
    y1_2 = [b_ref[:, tile(second[i])] + 2.0 * dot(x0[i], w[i][0, 1]) for i in both]
    y0_2 = [dot(x0[i], w[i][0, 0]) + share[i][K:] for i in both]
    far2 = [far2[i] + dot(x0[i], we[i]) for i in both]
    y0_2 = [b_ref[:, tile(outer[i])] + 2.0 * (y0_2[i] - center * y0_1[i]) for i in both]
    far2 = [got[i][2 * K :].astype(F32) + 2.0 * (far2[i] - center * far1[i]) for i in both]
    x1, x0, xf = [bf(y) for y in y1_2], [bf(y) for y in y0_2], [bf(f) for f in far2]
    y2_3 = [c_ref[:, tile(second[i])] + 2.0 * dot(x1[i], w[i][1, 2]) for i in both]
    y1_3 = [dot(x1[i], w[i][1, 1]) + dot(x0[i], w[i][0, 1]) for i in both]
    y0_3 = [dot(x1[i], w[i][1, 0]) + dot(x0[i], w[i][0, 0]) + dot(xf[i], wn[i]) for i in both]
    y1_3 = [c_ref[:, tile(outer[i])] + 2.0 * (y1_3[i] - center * y1_2[i]) for i in both]
    y0_3 = [2.0 * (y0_3[i] - center * y0_2[i]) - y0_1[i] for i in both]
    return list(zip(y0_2, y1_2)), list(zip(y0_3, y1_3, y2_3))


def edge3_kernel(
    last, re_ref, ro_ref, z_ref, o_ref, b_ref, c_ref, w_in, w_out, wn_ref, w_edge, fe_ref, fo_ref, *rest
):
    even = is_even()
    got = chosen(even, re_ref[...], ro_ref[...])
    far = chosen(even, fe_ref[...], fo_ref[...])
    e_ref = rest[1] if last else rest[0]
    both = range(2)
    w = [side_weights(i, w_in, w_out) for i in both]
    wn, we = [wn_ref[tile(i)] for i in both], [w_edge[tile(i)] for i in both]
    two, three = three_on(got, w, wn, far, we, z_ref, o_ref, b_ref, c_ref)
    for i in both:
        for n in range(3):
            e_ref[:, tile(5 - n if i else n)] = three[i][n]
    if not last:
        _, p_ref, zn_ref, _, _ = rest
        z, parts = prepare(w, three, [bf(y[2]) for y in three], two)
        for i in both:
            p_ref[:, tile(i)] = two[i][1]
            zn_ref[:, tile(i)] = z[i]
    if last:
        g = rest[0][...] + gram(e_ref[...])
        rest[2][...] = jnp.concatenate([g[: K // 2], g[K // 2 :]], axis=1)
    else:
        send(even, parts[0], parts[1], rest[3], rest[4])


def split(x):
    high = x.astype(BF16)
    rest = x - high.astype(F32)
    mid = rest.astype(BF16)
    return high, mid, (rest - mid.astype(F32)).astype(BF16)


def inverse_factor(g):
    row = lax.broadcasted_iota(jnp.int32, (K, K), 0)
    col = lax.broadcasted_iota(jnp.int32, (K, K), 1)
    whole = jnp.concatenate([g, (row == col).astype(F32)], axis=1)
    count = K // 8
    shape = (8, 2 * K)
    blocks = [whole[8 * i : 8 * i + 8] for i in range(count)]
    sub = lax.broadcasted_iota(jnp.int32, shape, 0)
    scaled = []
    for b in range(count):
        rows = [jnp.broadcast_to(blocks[b][a : a + 1], shape) for a in range(8)]
        entry = {
            (a, c): jnp.broadcast_to(rows[a][:, 8 * b + c : 8 * b + c + 1], shape)
            for a in range(8)
            for c in range(8)
        }
        columns = {
            i: [jnp.broadcast_to(blocks[i][:, 8 * b + c : 8 * b + c + 1], shape) for c in range(8)]
            for i in range(b + 1, count)
        }
        pivots, inverses = rows[0], None
        for a in range(8):
            inverse = 1.0 / entry[a, a]
            inverses = inverse if a == 0 else jnp.where(sub == a, inverse, inverses)
            if a > 0:
                pivots = jnp.where(sub == a, rows[a], pivots)
            for r in range(a + 1, 8):
                m = entry[r, a] * inverse
                rows[r] = rows[r] - m * rows[a]
                for c in range(a + 1, 8):
                    entry[r, c] = entry[r, c] - m * entry[a, c]
            for i in columns:
                m = columns[i][a] * inverse
                for c in range(a + 1, 8):
                    columns[i][c] = columns[i][c] - m * entry[a, c]
                columns[i][a] = m
        for i in columns:
            update = columns[i][0] * rows[0]
            for a in range(1, 8):
                update = update + columns[i][a] * rows[a]
            blocks[i] = blocks[i] - update
        scaled.append(pivots * jnp.sqrt(inverses))
    return jnp.concatenate(scaled, axis=0)[:, K:]


def whiten_kernel(scale, g_ref, e_ref, i_ref, out_ref, buf, sems):
    g = g_ref[...] * scale
    high, mid, low = split(inverse_factor(jnp.concatenate([g[:, :K], g[:, K:]], axis=0)))
    left = jnp.concatenate([high, mid, high, low, mid, high], axis=1)
    copies = []
    for n, (at, y) in enumerate(
        ((tile(0, 3), e_ref[:, tile(0, 3)]), (tile(3, 2), i_ref[...]), (tile(5, 3), e_ref[:, tile(3, 3)]))
    ):
        yh, ym, yl = split(y)
        right = jnp.concatenate([yh, yh, ym, yh, ym, yl], axis=0)
        buf[:, at] = dot(left, right)
        copy = pltpu.make_async_copy(buf.at[:, at], out_ref.at[:, at], sems.at[n])
        copy.start()
        copies.append(copy)
    for copy in copies:
        copy.wait()


def local(modes, tiles, tile_pair, boundary):
    count = lax.axis_size("slab") * lax.axis_size("col")
    pairs_even = [(i, i ^ 1) for i in range(count)]
    pairs_odd = [(i, (i + 1) % count if i % 2 else (i - 1) % count) for i in range(count)]

    def exchange(se, so):
        ro = lax.ppermute(so, AXES, pairs_odd)
        re = lax.ppermute(se, AXES, pairs_even)
        return re, ro

    def f32(tiles_wide):
        return pltpu.VMEM((K, tiles_wide * TB), F32)

    def weights(n):
        return pltpu.VMEM((n * TB, TB), BF16)

    def sends(rows):
        return pltpu.VMEM((rows, TB), BF16)

    w_out, w_edge, z, se, so, inv = pl.pallas_call(
        first_kernel,
        out_shape=(
            weights(4), weights(2), f32(2), sends(2 * K + TB), sends(2 * K + TB), pltpu.SMEM((TL,), jnp.int32),
        ),
        in_specs=[HBM, HBM, HBM, HBM],
        out_specs=(VM, VM, VM, VM, VM, SM),
        scratch_shapes=[
            pltpu.SMEM((TL,), jnp.int32),
            pltpu.SMEM((1, 2), jnp.int32),
            pltpu.VMEM((K, 4 * TB), F32),
            pltpu.SemaphoreType.DMA((8,)),
            pltpu.SemaphoreType.DMA((2,)),
        ],
        compiler_params=params(8),
        name="first",
    )(hbm(boundary), hbm(tile_pair), hbm(modes), hbm(tiles))
    re, ro = exchange(se, so)
    w_in, j, m, b, o, fe, fo = pl.pallas_call(
        load_kernel,
        out_shape=(weights(18), f32(6), f32(4), f32(4), f32(2), weights(1), weights(1)),
        in_specs=[SM, HBM, HBM, VM, VM],
        out_specs=(VM,) * 7,
        scratch_shapes=[
            pltpu.VMEM((K, ROWS), F32),
            pltpu.VMEM((K, ROWS), BF16),
            pltpu.VMEM((K, 6 * TB), BF16),
            pltpu.SemaphoreType.DMA((18,)),
            pltpu.SemaphoreType.DMA,
        ],
        compiler_params=params(12),
        cost_estimate=cost(40),
        name="load",
    )(inv, hbm(modes), hbm(tiles), pin(w_out), pin(w_edge))
    fe, fo, re = lax.optimization_barrier((fe, fo, re))
    fe, fo = exchange(fe, fo)
    e, z, se, so, wn = pl.pallas_call(
        edge2_kernel,
        out_shape=(f32(4), f32(2), sends(3 * K), sends(3 * K), weights(2)),
        in_specs=[VM] * 9,
        out_specs=(VM,) * 5,
        compiler_params=params(8),
        name="edge2",
    )(re, ro, pin(z), pin(o), pin(b), pin(w_in), pin(w_out), pin(m), pin(j))
    state = (e, m, j)
    for later in (False, True):
        re, ro = exchange(se, so)
        outs = pl.pallas_call(
            functools.partial(step_kernel, later, later),
            out_shape=(f32(4), f32(4), f32(2), f32(2), f32(4)) + ((pltpu.VMEM((K, K), F32),) if later else ()),
            in_specs=[VM] * (len(state) + 3),
            out_specs=(VM,) * (6 if later else 5),
            scratch_shapes=[
                pltpu.VMEM((K, ROWS), BF16),
                pltpu.VMEM((K, 6 * TB), BF16),
                pltpu.VMEM((K, 4 * TB), BF16),
                pltpu.VMEM((K, 6 * TB), F32),
            ],
            compiler_params=params(10),
            cost_estimate=cost(52),
            name="step",
        )(*(pin(x) for x in state), pin(w_in), pin(w_out), pin(w_edge))
        m, b, o, t, c = outs[:5]
        shared = (
            re, ro, pin(z), pin(o), pin(b), pin(c), pin(w_in), pin(w_out), pin(wn), pin(w_edge), fe, fo
        )
        if not later:
            e, p, z, se, so = pl.pallas_call(
                functools.partial(edge3_kernel, False),
                out_shape=(f32(6), f32(2), f32(2), sends(3 * K), sends(3 * K)),
                in_specs=[VM] * 12,
                out_specs=(VM,) * 5,
                compiler_params=params(8),
                name="edge3",
            )(*shared)
            state = (e, t, p, m)
    e, g = pl.pallas_call(
        functools.partial(edge3_kernel, True),
        out_shape=(f32(6), pltpu.VMEM((K // 2, 2 * K), F32)),
        in_specs=[VM] * 13,
        out_specs=(VM, VM),
        compiler_params=params(8),
        name="final",
    )(*shared, pin(outs[5]))
    for group in ((16,), (1, 3, 2), (4, 12, 8), (32, 96, 64)):
        got = [lax.ppermute(g, AXES, [(i, i ^ bits) for i in range(count)]) for bits in group]
        for other in got:
            g = g + other
    return pl.pallas_call(
        functools.partial(whiten_kernel, 1.0 / (ROWS * count)),
        out_shape=jax.ShapeDtypeStruct((K, ROWS), F32),
        in_specs=[VM, VM, VM],
        out_specs=HBM,
        scratch_shapes=[pltpu.VMEM((K, ROWS), F32), pltpu.SemaphoreType.DMA((3,))],
        compiler_params=params(16),
        name="whiten",
    )(g, pin(e), pin(t))


def solution(mesh):
    placed = (
        P(None, AXES),
        P(AXES, None, None),
        P(AXES),
        P(AXES, None),
    )
    return jax.shard_map(
        local, mesh=mesh, in_specs=placed, out_specs=P(None, AXES), check_vma=False
    )
```

```python
import functools

import jax
import jax.numpy as jnp
from jax import lax
from jax.experimental import pallas as pl
from jax.experimental.pallas import tpu as pltpu
from jax.sharding import PartitionSpec as P

DEG = 8
center = 0.25
AXES = ("slab", "col")
K = 64
TB = 384
RT = 8
TL = 24
ROWS = RT * TB
F32 = jnp.float32
BF16 = jnp.bfloat16

VM = pl.BlockSpec(memory_space=pltpu.VMEM)
SM = pl.BlockSpec(memory_space=pltpu.SMEM)
HBM = pl.BlockSpec(memory_space=pltpu.HBM)


def pin(x):
    return pltpu.with_memory_space_constraint(x, pltpu.VMEM)


def hbm(x):
    return pltpu.with_memory_space_constraint(x, pltpu.HBM)


def params(mib):
    return pltpu.CompilerParams(vmem_limit_bytes=mib << 20)


def cost(tile_products):
    return pl.CostEstimate(flops=2 * K * TB * TB * tile_products, bytes_accessed=8 << 20, transcendentals=0)


def dot(a, b):
    return jnp.dot(a, b, preferred_element_type=F32)


def is_even():
    return lax.rem(lax.axis_index("col"), 2) == 0


def tile(i, n=1):
    return slice(i * TB, (i + n) * TB)


OUTER = [1, 3, 20, 22]
INNER = [3 * c + (r - c) + 1 for r in range(1, RT - 1) for c in (r - 1, r, r + 1)]


def inner(r, first=0, count=3):
    return tile(3 * (r - 1) + first, count)


def first_kernel(
    bound_ref, pair_ref, modes_ref, tiles_ref,
    outer_ref, we_ref, z_ref, se_ref, so_ref, inv_ref,
    pair, bound, ym, sems, ssem,
):
    to_smem = pltpu.make_async_copy(pair_ref, pair, ssem.at[0])
    to_smem.start()
    bound_copy = pltpu.make_async_copy(bound_ref, bound, ssem.at[1])
    bound_copy.start()
    modes = [
        pltpu.make_async_copy(modes_ref.at[:, tile(0, 2)], ym.at[:, tile(0, 2)], sems.at[6]),
        pltpu.make_async_copy(modes_ref.at[:, tile(6, 2)], ym.at[:, tile(2, 2)], sems.at[7]),
    ]
    for c in modes:
        c.start()
    to_smem.wait()
    for t in range(TL):
        inv_ref[pair[t]] = t
    edge_copies = [
        pltpu.make_async_copy(tiles_ref.at[inv_ref[p]], we_ref.at[tile(i)], sems.at[4 + i])
        for i, p in enumerate((0, TL - 1))
    ]
    outer_copies = [
        pltpu.make_async_copy(tiles_ref.at[inv_ref[p]], outer_ref.at[tile(i)], sems.at[i])
        for i, p in enumerate(OUTER)
    ]
    for c in edge_copies + outer_copies:
        c.start()
    for c in modes:
        c.wait()
    xs = ym[...].astype(BF16)
    bound_copy.wait()
    for c in edge_copies:
        c.wait()
    row = lax.broadcasted_iota(jnp.int32, (TB, TB), 0)
    zero = jnp.zeros((TB, TB), BF16)
    w_low = jnp.where(row < bound[0, 0], we_ref[tile(0)], zero)
    w_high = jnp.where(row >= TB - bound[0, 1], we_ref[tile(1)], zero)
    we_ref[tile(0)] = w_low
    we_ref[tile(1)] = w_high
    even = is_even()
    se_ref[2 * K :] = jnp.where(even, w_high, w_low)
    so_ref[2 * K :] = jnp.where(even, w_low, w_high)
    for c in outer_copies:
        c.wait()
    z_low = dot(xs[:, tile(0, 2)], outer_ref[tile(0, 2)]) - center * ym[:, tile(0)]
    z_high = dot(xs[:, tile(2, 2)], outer_ref[tile(2, 2)]) - center * ym[:, tile(3)]
    z_ref[:, tile(0)] = z_low
    z_ref[:, tile(1)] = z_high
    send(even, (xs[:, tile(0)], z_low), (xs[:, tile(3)], z_high), se_ref, so_ref)


def send(even, low, high, se_ref, so_ref):
    for i, (a, b) in enumerate(zip(low, high)):
        a, b = a.astype(BF16), b.astype(BF16)
        se_ref[i * K : (i + 1) * K] = jnp.where(even, b, a)
        so_ref[i * K : (i + 1) * K] = jnp.where(even, a, b)


def one_on(factor, now, before, xs, w_in, xn, keep):
    for r in range(1, RT - 1):
        acc = dot(xs[:, tile(r - 1, 3)], w_in[inner(r)]) - center * now(r)
        value = acc if before is None else factor * acc - before(r)
        keep(r, value)
        xn[:, tile(r - 1)] = value.astype(BF16)


def two_on(now, one, xn, w_in, w_out, b_ref, keep):
    for r in range(2, RT - 2):
        acc = dot(xn[:, tile(r - 2, 3)], w_in[inner(r)]) - center * one(r)
        keep(r, 2.0 * acc - now(r))
    b_ref[:, tile(0)] = 2.0 * dot(xn[:, tile(0)], w_out[tile(1)]) - now(0)
    acc = dot(xn[:, tile(0, 2)], w_in[inner(1, 1, 2)]) - center * one(1)
    b_ref[:, tile(1)] = 2.0 * acc - now(1)
    acc = dot(xn[:, tile(4, 2)], w_in[inner(6, 0, 2)]) - center * one(6)
    b_ref[:, tile(2)] = 2.0 * acc - now(6)
    b_ref[:, tile(3)] = 2.0 * dot(xn[:, tile(5)], w_out[tile(2)]) - now(7)


def overflow(factor, xs, w_edge, o_ref):
    o_ref[:, tile(0)] = factor * dot(xs[:, tile(0)], w_edge[tile(0)])
    o_ref[:, tile(1)] = factor * dot(xs[:, tile(RT - 1)], w_edge[tile(1)])


def load_kernel(
    inv_ref, modes_ref, tiles_ref, w_out, w_edge,
    w_in, j_ref, m_ref, b_ref, o_ref, fe_ref, fo_ref,
    y0, xs, xn, sems, msem,
):
    mcopy = pltpu.make_async_copy(modes_ref, y0, msem)
    mcopy.start()
    copies = [
        pltpu.make_async_copy(tiles_ref.at[inv_ref[p]], w_in.at[tile(i)], sems.at[i])
        for i, p in enumerate(INNER)
    ]
    for c in copies:
        c.start()
    mcopy.wait()
    for c in copies:
        c.wait()
    xs[...] = y0[...].astype(BF16)
    even = is_even()
    w_low, w_high = w_out[tile(0)], w_out[tile(3)]
    fe_ref[...] = jnp.where(even, w_high, w_low)
    fo_ref[...] = jnp.where(even, w_low, w_high)

    def keep_one(r, value):
        j_ref[:, tile(r - 1)] = value

    def keep_two(r, value):
        m_ref[:, tile(r - 2)] = value

    def now(r):
        return y0[:, tile(r)]

    one_on(1.0, now, None, xs, w_in, xn, keep_one)
    overflow(1.0, xs, w_edge, o_ref)
    two_on(now, lambda r: j_ref[:, tile(r - 1)], xn, w_in, w_out, b_ref, keep_two)


def step_kernel(later, last, *refs):
    if later:
        e_ref, n_ref, p_ref, q_ref = refs[:4]
    else:
        e_ref, n_ref, p_ref = refs[:3]
    w_in, w_out, w_edge, m_ref, b_ref, o_ref, t_ref, c_ref, *rest = refs[4 if later else 3 :]
    xs, xn, xm, one_ref = rest[-4:]
    edge = 3 if later else 2

    def now(r):
        if r < edge:
            return e_ref[:, tile(r)]
        if r >= RT - edge:
            return e_ref[:, tile(r - RT + 2 * edge)]
        return n_ref[:, tile(r - edge)]

    def before(r):
        if not later:
            return p_ref[:, tile(r - 1)]
        if r in (1, 6):
            return p_ref[:, tile(0 if r == 1 else 1)]
        return q_ref[:, tile(r - 2)]

    def one(r):
        return one_ref[:, tile(r - 1)]

    def keep_one(r, value):
        one_ref[:, tile(r - 1)] = value

    def keep_two(r, value):
        m_ref[:, tile(r - 2)] = value
        xm[:, tile(r - 2)] = value.astype(BF16)

    for r in range(RT):
        xs[:, tile(r)] = now(r).astype(BF16)
    one_on(2.0, now, before, xs, w_in, xn, keep_one)
    overflow(2.0, xs, w_edge, o_ref)
    two_on(now, one, xn, w_in, w_out, b_ref, keep_two)
    for r in (3, 4):
        acc = dot(xm[:, tile(r - 3, 3)], w_in[inner(r)]) - center * m_ref[:, tile(r - 2)]
        t_ref[:, tile(r - 3)] = 2.0 * acc - one(r)
    c_ref[:, tile(0)] = 2.0 * dot(xm[:, tile(0)], w_in[inner(1, 2, 1)]) - one(1)
    acc = dot(xm[:, tile(0, 2)], w_in[inner(2, 1, 2)]) - center * m_ref[:, tile(0)]
    c_ref[:, tile(1)] = 2.0 * acc - one(2)
    acc = dot(xm[:, tile(2, 2)], w_in[inner(5, 0, 2)]) - center * m_ref[:, tile(3)]
    c_ref[:, tile(2)] = 2.0 * acc - one(5)
    c_ref[:, tile(3)] = 2.0 * dot(xm[:, tile(3)], w_in[inner(6, 0, 1)]) - one(6)
    if last:
        rest[0][...] = gram(t_ref[...])


def gram(y):
    parts = jnp.concatenate(split(y), axis=0)
    p = lax.dot_general(parts, parts, (((1,), (1,)), ((), ())), preferred_element_type=F32)

    def block(a, b):
        return p[a * K : (a + 1) * K, b * K : (b + 1) * K]

    small = block(1, 1) + (block(0, 2) + block(2, 0))
    return block(0, 0) + ((block(0, 1) + block(1, 0)) + small)


def bf(x):
    return x.astype(BF16)


def side_weights(side, w_in, w_out):
    if side == 0:
        rows = {(0, 0): w_out[tile(0)], (1, 0): w_out[tile(1)]}
        near, far = (0, 1, 2), (0, 1, 2)
    else:
        rows = {(0, 0): w_out[tile(3)], (1, 0): w_out[tile(2)]}
        near, far = (2, 1, 0), (2, 1, 0)
    first, second = (1, 2) if side == 0 else (6, 5)
    for source in range(3):
        rows[source, 1] = w_in[inner(first, near[source], 1)]
    rows[1, 2] = w_in[inner(second, far[0], 1)]
    return rows


def chosen(even, re, ro):
    return jnp.where(even, ro, re), jnp.where(even, re, ro)


def prepare(ws, ys, x2s, before):
    both = range(2)
    x = [[bf(y) for y in ys[i][:2]] for i in both]
    next1 = [dot(x[i][1], ws[i][1, 1]) + dot(x2s[i], ws[i][2, 1]) for i in both]
    next1 = [next1[i] + dot(x[i][0], ws[i][0, 1]) for i in both]
    next1 = [bf(2.0 * (next1[i] - center * ys[i][1]) - before[i][1]) for i in both]
    z = [dot(x[i][0], ws[i][0, 0]) + dot(x[i][1], ws[i][1, 0]) for i in both]
    s = [2.0 * dot(next1[i], ws[i][1, 0]) - ys[i][0] for i in both]
    z = [2.0 * (z[i] - center * ys[i][0]) - before[i][0] for i in both]
    return z, [(x[i][0], z[i], s[i]) for i in both]


def edge2_kernel(
    re_ref, ro_ref, z_ref, o_ref, b_ref, w_in, w_out, m_ref, j_ref,
    e_ref, zn_ref, se_ref, so_ref, wn_ref,
):
    even = is_even()
    got = chosen(even, re_ref[: 2 * K], ro_ref[: 2 * K])
    for side, w in enumerate(chosen(even, re_ref[2 * K :], ro_ref[2 * K :])):
        wn_ref[tile(side)] = w
    both = range(2)
    w = [side_weights(i, w_in, w_out) for i in both]
    wn = [wn_ref[tile(i)] for i in both]
    outer, second = (0, 3), (1, 2)
    far = [bf(got[i][K:].astype(F32) + o_ref[:, tile(i)]) for i in both]
    share = [dot(jnp.concatenate([got[i][:K], far[i]], axis=0), wn[i]) for i in both]
    y0_1 = [z_ref[:, tile(i)] + share[i][:K] for i in both]
    x0_1 = [bf(y) for y in y0_1]
    y1 = [b_ref[:, tile(second[i])] + 2.0 * dot(x0_1[i], w[i][0, 1]) for i in both]
    y0 = [dot(x0_1[i], w[i][0, 0]) + share[i][K:] for i in both]
    y0 = [b_ref[:, tile(outer[i])] + 2.0 * (y0[i] - center * y0_1[i]) for i in both]
    for i in both:
        e_ref[:, tile(outer[i])] = y0[i]
        e_ref[:, tile(second[i])] = y1[i]
    x2 = [bf(m_ref[:, tile(3 * i)]) for i in both]
    before = [(y0_1[i], j_ref[:, tile(5 * i)]) for i in both]
    z, parts = prepare(w, [(y0[i], y1[i]) for i in both], x2, before)
    for i in both:
        zn_ref[:, tile(i)] = z[i]
    send(even, parts[0], parts[1], se_ref, so_ref)


def three_on(got, w, wn, wf, we, z_ref, o_ref, b_ref, c_ref):
    both = range(2)
    outer, second = (0, 3), (1, 2)
    far1 = [got[i][K : 2 * K].astype(F32) + o_ref[:, tile(i)] for i in both]
    xf = [bf(f) for f in far1]
    share = [dot(jnp.concatenate([got[i][:K], xf[i]], axis=0), wn[i]) for i in both]
    y0_1 = [z_ref[:, tile(i)] + 2.0 * share[i][:K] for i in both]
    x0 = [bf(y) for y in y0_1]
    far2 = [dot(xf[i], wf[i]) for i in both]
    y1_2 = [b_ref[:, tile(second[i])] + 2.0 * dot(x0[i], w[i][0, 1]) for i in both]
    y0_2 = [dot(x0[i], w[i][0, 0]) + share[i][K:] for i in both]
    far2 = [far2[i] + dot(x0[i], we[i]) for i in both]
    y0_2 = [b_ref[:, tile(outer[i])] + 2.0 * (y0_2[i] - center * y0_1[i]) for i in both]
    far2 = [got[i][2 * K :].astype(F32) + 2.0 * (far2[i] - center * far1[i]) for i in both]
    x1, x0, xf = [bf(y) for y in y1_2], [bf(y) for y in y0_2], [bf(f) for f in far2]
    y2_3 = [c_ref[:, tile(second[i])] + 2.0 * dot(x1[i], w[i][1, 2]) for i in both]
    y1_3 = [dot(x1[i], w[i][1, 1]) + dot(x0[i], w[i][0, 1]) for i in both]
    y0_3 = [dot(x1[i], w[i][1, 0]) + dot(x0[i], w[i][0, 0]) + dot(xf[i], wn[i]) for i in both]
    y1_3 = [c_ref[:, tile(outer[i])] + 2.0 * (y1_3[i] - center * y1_2[i]) for i in both]
    y0_3 = [2.0 * (y0_3[i] - center * y0_2[i]) - y0_1[i] for i in both]
    return list(zip(y0_2, y1_2)), list(zip(y0_3, y1_3, y2_3))


def edge3_kernel(
    last, re_ref, ro_ref, z_ref, o_ref, b_ref, c_ref, w_in, w_out, wn_ref, w_edge, fe_ref, fo_ref, *rest
):
    even = is_even()
    got = chosen(even, re_ref[...], ro_ref[...])
    far = chosen(even, fe_ref[...], fo_ref[...])
    e_ref = rest[1] if last else rest[0]
    both = range(2)
    w = [side_weights(i, w_in, w_out) for i in both]
    wn, we = [wn_ref[tile(i)] for i in both], [w_edge[tile(i)] for i in both]
    two, three = three_on(got, w, wn, far, we, z_ref, o_ref, b_ref, c_ref)
    for i in both:
        for n in range(3):
            e_ref[:, tile(5 - n if i else n)] = three[i][n]
    if not last:
        _, p_ref, zn_ref, _, _ = rest
        z, parts = prepare(w, three, [bf(y[2]) for y in three], two)
        for i in both:
            p_ref[:, tile(i)] = two[i][1]
            zn_ref[:, tile(i)] = z[i]
    if last:
        g = rest[0][...] + gram(e_ref[...])
        rest[2][...] = jnp.concatenate([g[: K // 2], g[K // 2 :]], axis=1)
    else:
        send(even, parts[0], parts[1], rest[3], rest[4])


def split(x):
    high = x.astype(BF16)
    rest = x - high.astype(F32)
    mid = rest.astype(BF16)
    return high, mid, (rest - mid.astype(F32)).astype(BF16)


def inverse_factor(g):
    row = lax.broadcasted_iota(jnp.int32, (K, K), 0)
    col = lax.broadcasted_iota(jnp.int32, (K, K), 1)
    whole = jnp.concatenate([g, (row == col).astype(F32)], axis=1)
    count = K // 8
    shape = (8, 2 * K)
    blocks = [whole[8 * i : 8 * i + 8] for i in range(count)]
    sub = lax.broadcasted_iota(jnp.int32, shape, 0)
    scaled = []
    for b in range(count):
        rows = [jnp.broadcast_to(blocks[b][a : a + 1], shape) for a in range(8)]
        entry = {
            (a, c): jnp.broadcast_to(rows[a][:, 8 * b + c : 8 * b + c + 1], shape)
            for a in range(8)
            for c in range(8)
        }
        columns = {
            i: [jnp.broadcast_to(blocks[i][:, 8 * b + c : 8 * b + c + 1], shape) for c in range(8)]
            for i in range(b + 1, count)
        }
        pivots, inverses = rows[0], None
        for a in range(8):
            inverse = 1.0 / entry[a, a]
            inverses = inverse if a == 0 else jnp.where(sub == a, inverse, inverses)
            if a > 0:
                pivots = jnp.where(sub == a, rows[a], pivots)
            for r in range(a + 1, 8):
                m = entry[r, a] * inverse
                rows[r] = rows[r] - m * rows[a]
                for c in range(a + 1, 8):
                    entry[r, c] = entry[r, c] - m * entry[a, c]
            for i in columns:
                m = columns[i][a] * inverse
                for c in range(a + 1, 8):
                    columns[i][c] = columns[i][c] - m * entry[a, c]
                columns[i][a] = m
        for i in columns:
            update = columns[i][0] * rows[0]
            for a in range(1, 8):
                update = update + columns[i][a] * rows[a]
            blocks[i] = blocks[i] - update
        scaled.append(pivots * jnp.sqrt(inverses))
    return jnp.concatenate(scaled, axis=0)[:, K:]


def whiten_kernel(scale, g_ref, e_ref, i_ref, out_ref, buf, sems):
    g = g_ref[...] * scale
    high, mid, low = split(inverse_factor(jnp.concatenate([g[:, :K], g[:, K:]], axis=0)))
    left = jnp.concatenate([high, mid, high, low, mid, high], axis=1)
    copies = []
    for n, (at, y) in enumerate(
        ((tile(0, 3), e_ref[:, tile(0, 3)]), (tile(3, 2), i_ref[...]), (tile(5, 3), e_ref[:, tile(3, 3)]))
    ):
        yh, ym, yl = split(y)
        right = jnp.concatenate([yh, yh, ym, yh, ym, yl], axis=0)
        buf[:, at] = dot(left, right)
        copy = pltpu.make_async_copy(buf.at[:, at], out_ref.at[:, at], sems.at[n])
        copy.start()
        copies.append(copy)
    for copy in copies:
        copy.wait()


def local(modes, tiles, tile_pair, boundary):
    count = lax.axis_size("slab") * lax.axis_size("col")
    pairs_even = [(i, i ^ 1) for i in range(count)]
    pairs_odd = [(i, (i + 1) % count if i % 2 else (i - 1) % count) for i in range(count)]

    def exchange(se, so):
        ro = lax.ppermute(so, AXES, pairs_odd)
        re = lax.ppermute(se, AXES, pairs_even)
        return re, ro

    def f32(tiles_wide):
        return pltpu.VMEM((K, tiles_wide * TB), F32)

    def weights(n):
        return pltpu.VMEM((n * TB, TB), BF16)

    def sends(rows):
        return pltpu.VMEM((rows, TB), BF16)

    w_out, w_edge, z, se, so, inv = pl.pallas_call(
        first_kernel,
        out_shape=(
            weights(4), weights(2), f32(2), sends(2 * K + TB), sends(2 * K + TB), pltpu.SMEM((TL,), jnp.int32),
        ),
        in_specs=[HBM, HBM, HBM, HBM],
        out_specs=(VM, VM, VM, VM, VM, SM),
        scratch_shapes=[
            pltpu.SMEM((TL,), jnp.int32),
            pltpu.SMEM((1, 2), jnp.int32),
            pltpu.VMEM((K, 4 * TB), F32),
            pltpu.SemaphoreType.DMA((8,)),
            pltpu.SemaphoreType.DMA((2,)),
        ],
        compiler_params=params(8),
        name="first",
    )(hbm(boundary), hbm(tile_pair), hbm(modes), hbm(tiles))
    re, ro = exchange(se, so)
    w_in, j, m, b, o, fe, fo = pl.pallas_call(
        load_kernel,
        out_shape=(weights(18), f32(6), f32(4), f32(4), f32(2), weights(1), weights(1)),
        in_specs=[SM, HBM, HBM, VM, VM],
        out_specs=(VM,) * 7,
        scratch_shapes=[
            pltpu.VMEM((K, ROWS), F32),
            pltpu.VMEM((K, ROWS), BF16),
            pltpu.VMEM((K, 6 * TB), BF16),
            pltpu.SemaphoreType.DMA((18,)),
            pltpu.SemaphoreType.DMA,
        ],
        compiler_params=params(12),
        cost_estimate=cost(40),
        name="load",
    )(inv, hbm(modes), hbm(tiles), pin(w_out), pin(w_edge))
    fo, re = lax.optimization_barrier((fo, re))
    fe, fo = exchange(fe, fo)
    e, z, se, so, wn = pl.pallas_call(
        edge2_kernel,
        out_shape=(f32(4), f32(2), sends(3 * K), sends(3 * K), weights(2)),
        in_specs=[VM] * 9,
        out_specs=(VM,) * 5,
        compiler_params=params(8),
        name="edge2",
    )(re, ro, pin(z), pin(o), pin(b), pin(w_in), pin(w_out), pin(m), pin(j))
    state = (e, m, j)
    for later in (False, True):
        re, ro = exchange(se, so)
        outs = pl.pallas_call(
            functools.partial(step_kernel, later, later),
            out_shape=(f32(4), f32(4), f32(2), f32(2), f32(4)) + ((pltpu.VMEM((K, K), F32),) if later else ()),
            in_specs=[VM] * (len(state) + 3),
            out_specs=(VM,) * (6 if later else 5),
            scratch_shapes=[
                pltpu.VMEM((K, ROWS), BF16),
                pltpu.VMEM((K, 6 * TB), BF16),
                pltpu.VMEM((K, 4 * TB), BF16),
                pltpu.VMEM((K, 6 * TB), F32),
            ],
            compiler_params=params(10),
            cost_estimate=cost(52),
            name="step",
        )(*(pin(x) for x in state), pin(w_in), pin(w_out), pin(w_edge))
        m, b, o, t, c = outs[:5]
        shared = (
            re, ro, pin(z), pin(o), pin(b), pin(c), pin(w_in), pin(w_out), pin(wn), pin(w_edge), fe, fo
        )
        if not later:
            e, p, z, se, so = pl.pallas_call(
                functools.partial(edge3_kernel, False),
                out_shape=(f32(6), f32(2), f32(2), sends(3 * K), sends(3 * K)),
                in_specs=[VM] * 12,
                out_specs=(VM,) * 5,
                compiler_params=params(8),
                name="edge3",
            )(*shared)
            state = (e, t, p, m)
    e, g = pl.pallas_call(
        functools.partial(edge3_kernel, True),
        out_shape=(f32(6), pltpu.VMEM((K // 2, 2 * K), F32)),
        in_specs=[VM] * 13,
        out_specs=(VM, VM),
        compiler_params=params(8),
        name="final",
    )(*shared, pin(outs[5]))
    for group in ((16,), (1, 3, 2), (4, 12, 8), (32, 96, 64)):
        got = [lax.ppermute(g, AXES, [(i, i ^ bits) for i in range(count)]) for bits in group]
        for other in got:
            g = g + other
    return pl.pallas_call(
        functools.partial(whiten_kernel, 1.0 / (ROWS * count)),
        out_shape=jax.ShapeDtypeStruct((K, ROWS), F32),
        in_specs=[VM, VM, VM],
        out_specs=HBM,
        scratch_shapes=[pltpu.VMEM((K, ROWS), F32), pltpu.SemaphoreType.DMA((3,))],
        compiler_params=params(16),
        name="whiten",
    )(g, pin(e), pin(t))


def solution(mesh):
    placed = (
        P(None, AXES),
        P(AXES, None, None),
        P(AXES),
        P(AXES, None),
    )
    return jax.shard_map(
        local, mesh=mesh, in_specs=placed, out_specs=P(None, AXES), check_vma=False
    )
```

```python
import functools

import jax
import jax.numpy as jnp
from jax import lax
from jax.experimental import pallas as pl
from jax.experimental.pallas import tpu as pltpu
from jax.sharding import PartitionSpec as P

DEG = 8
center = 0.25
AXES = ("slab", "col")
K = 64
TB = 384
RT = 8
TL = 24
ROWS = RT * TB
F32 = jnp.float32
BF16 = jnp.bfloat16

VM = pl.BlockSpec(memory_space=pltpu.VMEM)
SM = pl.BlockSpec(memory_space=pltpu.SMEM)
HBM = pl.BlockSpec(memory_space=pltpu.HBM)


def pin(x):
    return pltpu.with_memory_space_constraint(x, pltpu.VMEM)


def hbm(x):
    return pltpu.with_memory_space_constraint(x, pltpu.HBM)


def params(mib):
    return pltpu.CompilerParams(vmem_limit_bytes=mib << 20)


def cost(tile_products):
    return pl.CostEstimate(flops=2 * K * TB * TB * tile_products, bytes_accessed=8 << 20, transcendentals=0)


def dot(a, b):
    return jnp.dot(a, b, preferred_element_type=F32)


def is_even():
    return lax.rem(lax.axis_index("col"), 2) == 0


def tile(i, n=1):
    return slice(i * TB, (i + n) * TB)


OUTER = [1, 3, 20, 22]
INNER = [3 * c + (r - c) + 1 for r in range(1, RT - 1) for c in (r - 1, r, r + 1)]


def inner(r, first=0, count=3):
    return tile(3 * (r - 1) + first, count)


def first_kernel(
    bound_ref, pair_ref, modes_ref, tiles_ref,
    outer_ref, we_ref, z_ref, se_ref, so_ref, inv_ref,
    pair, bound, ym, sems, ssem,
):
    to_smem = pltpu.make_async_copy(pair_ref, pair, ssem.at[0])
    to_smem.start()
    bound_copy = pltpu.make_async_copy(bound_ref, bound, ssem.at[1])
    bound_copy.start()
    modes = [
        pltpu.make_async_copy(modes_ref.at[:, tile(0, 2)], ym.at[:, tile(0, 2)], sems.at[6]),
        pltpu.make_async_copy(modes_ref.at[:, tile(6, 2)], ym.at[:, tile(2, 2)], sems.at[7]),
    ]
    for c in modes:
        c.start()
    to_smem.wait()
    for t in range(TL):
        inv_ref[pair[t]] = t
    edge_copies = [
        pltpu.make_async_copy(tiles_ref.at[inv_ref[p]], we_ref.at[tile(i)], sems.at[4 + i])
        for i, p in enumerate((0, TL - 1))
    ]
    outer_copies = [
        pltpu.make_async_copy(tiles_ref.at[inv_ref[p]], outer_ref.at[tile(i)], sems.at[i])
        for i, p in enumerate(OUTER)
    ]
    for c in edge_copies + outer_copies:
        c.start()
    for c in modes:
        c.wait()
    xs = ym[...].astype(BF16)
    bound_copy.wait()
    for c in edge_copies:
        c.wait()
    row = lax.broadcasted_iota(jnp.int32, (TB, TB), 0)
    zero = jnp.zeros((TB, TB), BF16)
    w_low = jnp.where(row < bound[0, 0], we_ref[tile(0)], zero)
    w_high = jnp.where(row >= TB - bound[0, 1], we_ref[tile(1)], zero)
    we_ref[tile(0)] = w_low
    we_ref[tile(1)] = w_high
    even = is_even()
    se_ref[2 * K :] = jnp.where(even, w_high, w_low)
    so_ref[2 * K :] = jnp.where(even, w_low, w_high)
    for c in outer_copies:
        c.wait()
    z_low = dot(xs[:, tile(0, 2)], outer_ref[tile(0, 2)]) - center * ym[:, tile(0)]
    z_high = dot(xs[:, tile(2, 2)], outer_ref[tile(2, 2)]) - center * ym[:, tile(3)]
    z_ref[:, tile(0)] = z_low
    z_ref[:, tile(1)] = z_high
    send(even, (xs[:, tile(0)], z_low), (xs[:, tile(3)], z_high), se_ref, so_ref)


def send(even, low, high, se_ref, so_ref):
    for i, (a, b) in enumerate(zip(low, high)):
        a, b = a.astype(BF16), b.astype(BF16)
        se_ref[i * K : (i + 1) * K] = jnp.where(even, b, a)
        so_ref[i * K : (i + 1) * K] = jnp.where(even, a, b)


def one_on(factor, now, before, xs, w_in, xn, keep):
    for r in range(1, RT - 1):
        acc = dot(xs[:, tile(r - 1, 3)], w_in[inner(r)]) - center * now(r)
        value = acc if before is None else factor * acc - before(r)
        keep(r, value)
        xn[:, tile(r - 1)] = value.astype(BF16)


def two_on(now, one, xn, w_in, w_out, b_ref, keep):
    for r in range(2, RT - 2):
        acc = dot(xn[:, tile(r - 2, 3)], w_in[inner(r)]) - center * one(r)
        keep(r, 2.0 * acc - now(r))
    b_ref[:, tile(0)] = 2.0 * dot(xn[:, tile(0)], w_out[tile(1)]) - now(0)
    acc = dot(xn[:, tile(0, 2)], w_in[inner(1, 1, 2)]) - center * one(1)
    b_ref[:, tile(1)] = 2.0 * acc - now(1)
    acc = dot(xn[:, tile(4, 2)], w_in[inner(6, 0, 2)]) - center * one(6)
    b_ref[:, tile(2)] = 2.0 * acc - now(6)
    b_ref[:, tile(3)] = 2.0 * dot(xn[:, tile(5)], w_out[tile(2)]) - now(7)


def overflow(factor, xs, w_edge, o_ref):
    o_ref[:, tile(0)] = factor * dot(xs[:, tile(0)], w_edge[tile(0)])
    o_ref[:, tile(1)] = factor * dot(xs[:, tile(RT - 1)], w_edge[tile(1)])


def load_kernel(
    inv_ref, modes_ref, tiles_ref, w_out, w_edge,
    w_in, j_ref, m_ref, b_ref, o_ref, fe_ref, fo_ref,
    y0, xs, xn, sems, msem,
):
    mcopy = pltpu.make_async_copy(modes_ref, y0, msem)
    mcopy.start()
    copies = [
        pltpu.make_async_copy(tiles_ref.at[inv_ref[p]], w_in.at[tile(i)], sems.at[i])
        for i, p in enumerate(INNER)
    ]
    for c in copies:
        c.start()
    mcopy.wait()
    for c in copies:
        c.wait()
    xs[...] = y0[...].astype(BF16)
    even = is_even()
    w_low, w_high = w_out[tile(0)], w_out[tile(3)]
    fe_ref[...] = jnp.where(even, w_high, w_low)
    fo_ref[...] = jnp.where(even, w_low, w_high)

    def keep_one(r, value):
        j_ref[:, tile(r - 1)] = value

    def keep_two(r, value):
        m_ref[:, tile(r - 2)] = value

    def now(r):
        return y0[:, tile(r)]

    one_on(1.0, now, None, xs, w_in, xn, keep_one)
    overflow(1.0, xs, w_edge, o_ref)
    two_on(now, lambda r: j_ref[:, tile(r - 1)], xn, w_in, w_out, b_ref, keep_two)


def step_kernel(later, last, *refs):
    if later:
        e_ref, n_ref, p_ref, q_ref = refs[:4]
    else:
        e_ref, n_ref, p_ref = refs[:3]
    w_in, w_out, w_edge, m_ref, b_ref, o_ref, t_ref, c_ref, *rest = refs[4 if later else 3 :]
    xs, xn, xm, one_ref = rest[-4:]
    edge = 3 if later else 2

    def now(r):
        if r < edge:
            return e_ref[:, tile(r)]
        if r >= RT - edge:
            return e_ref[:, tile(r - RT + 2 * edge)]
        return n_ref[:, tile(r - edge)]

    def before(r):
        if not later:
            return p_ref[:, tile(r - 1)]
        if r in (1, 6):
            return p_ref[:, tile(0 if r == 1 else 1)]
        return q_ref[:, tile(r - 2)]

    def one(r):
        return one_ref[:, tile(r - 1)]

    def keep_one(r, value):
        one_ref[:, tile(r - 1)] = value

    def keep_two(r, value):
        m_ref[:, tile(r - 2)] = value
        xm[:, tile(r - 2)] = value.astype(BF16)

    for r in range(RT):
        xs[:, tile(r)] = now(r).astype(BF16)
    one_on(2.0, now, before, xs, w_in, xn, keep_one)
    overflow(2.0, xs, w_edge, o_ref)
    two_on(now, one, xn, w_in, w_out, b_ref, keep_two)
    for r in (3, 4):
        acc = dot(xm[:, tile(r - 3, 3)], w_in[inner(r)]) - center * m_ref[:, tile(r - 2)]
        t_ref[:, tile(r - 3)] = 2.0 * acc - one(r)
    c_ref[:, tile(0)] = 2.0 * dot(xm[:, tile(0)], w_in[inner(1, 2, 1)]) - one(1)
    acc = dot(xm[:, tile(0, 2)], w_in[inner(2, 1, 2)]) - center * m_ref[:, tile(0)]
    c_ref[:, tile(1)] = 2.0 * acc - one(2)
    acc = dot(xm[:, tile(2, 2)], w_in[inner(5, 0, 2)]) - center * m_ref[:, tile(3)]
    c_ref[:, tile(2)] = 2.0 * acc - one(5)
    c_ref[:, tile(3)] = 2.0 * dot(xm[:, tile(3)], w_in[inner(6, 0, 1)]) - one(6)
    if last:
        rest[0][...] = gram(t_ref[...])


def gram(y):
    parts = jnp.concatenate(split(y), axis=0)
    p = lax.dot_general(parts, parts, (((1,), (1,)), ((), ())), preferred_element_type=F32)

    def block(a, b):
        return p[a * K : (a + 1) * K, b * K : (b + 1) * K]

    small = block(1, 1) + (block(0, 2) + block(2, 0))
    return block(0, 0) + ((block(0, 1) + block(1, 0)) + small)


def bf(x):
    return x.astype(BF16)


def side_weights(side, w_in, w_out):
    if side == 0:
        rows = {(0, 0): w_out[tile(0)], (1, 0): w_out[tile(1)]}
        near, far = (0, 1, 2), (0, 1, 2)
    else:
        rows = {(0, 0): w_out[tile(3)], (1, 0): w_out[tile(2)]}
        near, far = (2, 1, 0), (2, 1, 0)
    first, second = (1, 2) if side == 0 else (6, 5)
    for source in range(3):
        rows[source, 1] = w_in[inner(first, near[source], 1)]
    rows[1, 2] = w_in[inner(second, far[0], 1)]
    return rows


def chosen(even, re, ro):
    return jnp.where(even, ro, re), jnp.where(even, re, ro)


def prepare(ws, ys, x2s, before):
    both = range(2)
    x = [[bf(y) for y in ys[i][:2]] for i in both]
    next1 = [dot(x[i][1], ws[i][1, 1]) + dot(x2s[i], ws[i][2, 1]) for i in both]
    next1 = [next1[i] + dot(x[i][0], ws[i][0, 1]) for i in both]
    next1 = [bf(2.0 * (next1[i] - center * ys[i][1]) - before[i][1]) for i in both]
    z = [dot(x[i][0], ws[i][0, 0]) + dot(x[i][1], ws[i][1, 0]) for i in both]
    s = [2.0 * dot(next1[i], ws[i][1, 0]) - ys[i][0] for i in both]
    z = [2.0 * (z[i] - center * ys[i][0]) - before[i][0] for i in both]
    return z, [(x[i][0], z[i], s[i]) for i in both]


def edge2_kernel(
    re_ref, ro_ref, z_ref, o_ref, b_ref, w_in, w_out, m_ref, j_ref,
    e_ref, zn_ref, se_ref, so_ref, wn_ref,
):
    even = is_even()
    got = chosen(even, re_ref[: 2 * K], ro_ref[: 2 * K])
    for side, w in enumerate(chosen(even, re_ref[2 * K :], ro_ref[2 * K :])):
        wn_ref[tile(side)] = w
    both = range(2)
    w = [side_weights(i, w_in, w_out) for i in both]
    wn = [wn_ref[tile(i)] for i in both]
    outer, second = (0, 3), (1, 2)
    far = [bf(got[i][K:].astype(F32) + o_ref[:, tile(i)]) for i in both]
    share = [dot(jnp.concatenate([got[i][:K], far[i]], axis=0), wn[i]) for i in both]
    y0_1 = [z_ref[:, tile(i)] + share[i][:K] for i in both]
    x0_1 = [bf(y) for y in y0_1]
    y1 = [b_ref[:, tile(second[i])] + 2.0 * dot(x0_1[i], w[i][0, 1]) for i in both]
    y0 = [dot(x0_1[i], w[i][0, 0]) + share[i][K:] for i in both]
    y0 = [b_ref[:, tile(outer[i])] + 2.0 * (y0[i] - center * y0_1[i]) for i in both]
    for i in both:
        e_ref[:, tile(outer[i])] = y0[i]
        e_ref[:, tile(second[i])] = y1[i]
    x2 = [bf(m_ref[:, tile(3 * i)]) for i in both]
    before = [(y0_1[i], j_ref[:, tile(5 * i)]) for i in both]
    z, parts = prepare(w, [(y0[i], y1[i]) for i in both], x2, before)
    for i in both:
        zn_ref[:, tile(i)] = z[i]
    send(even, parts[0], parts[1], se_ref, so_ref)


def three_on(got, w, wn, wf, we, z_ref, o_ref, b_ref, c_ref):
    both = range(2)
    outer, second = (0, 3), (1, 2)
    far1 = [got[i][K : 2 * K].astype(F32) + o_ref[:, tile(i)] for i in both]
    xf = [bf(f) for f in far1]
    share = [dot(jnp.concatenate([got[i][:K], xf[i]], axis=0), wn[i]) for i in both]
    y0_1 = [z_ref[:, tile(i)] + 2.0 * share[i][:K] for i in both]
    x0 = [bf(y) for y in y0_1]
    far2 = [dot(xf[i], wf[i]) for i in both]
    y1_2 = [b_ref[:, tile(second[i])] + 2.0 * dot(x0[i], w[i][0, 1]) for i in both]
    y0_2 = [dot(x0[i], w[i][0, 0]) + share[i][K:] for i in both]
    far2 = [far2[i] + dot(x0[i], we[i]) for i in both]
    y0_2 = [b_ref[:, tile(outer[i])] + 2.0 * (y0_2[i] - center * y0_1[i]) for i in both]
    far2 = [got[i][2 * K :].astype(F32) + 2.0 * (far2[i] - center * far1[i]) for i in both]
    x1, x0, xf = [bf(y) for y in y1_2], [bf(y) for y in y0_2], [bf(f) for f in far2]
    y2_3 = [c_ref[:, tile(second[i])] + 2.0 * dot(x1[i], w[i][1, 2]) for i in both]
    y1_3 = [dot(x1[i], w[i][1, 1]) + dot(x0[i], w[i][0, 1]) for i in both]
    y0_3 = [dot(x1[i], w[i][1, 0]) + dot(x0[i], w[i][0, 0]) + dot(xf[i], wn[i]) for i in both]
    y1_3 = [c_ref[:, tile(outer[i])] + 2.0 * (y1_3[i] - center * y1_2[i]) for i in both]
    y0_3 = [2.0 * (y0_3[i] - center * y0_2[i]) - y0_1[i] for i in both]
    return list(zip(y0_2, y1_2)), list(zip(y0_3, y1_3, y2_3))


def edge3_kernel(
    last, re_ref, ro_ref, z_ref, o_ref, b_ref, c_ref, w_in, w_out, wn_ref, w_edge, fe_ref, fo_ref, *rest
):
    even = is_even()
    got = chosen(even, re_ref[...], ro_ref[...])
    far = chosen(even, fe_ref[...], fo_ref[...])
    e_ref = rest[1] if last else rest[0]
    both = range(2)
    w = [side_weights(i, w_in, w_out) for i in both]
    wn, we = [wn_ref[tile(i)] for i in both], [w_edge[tile(i)] for i in both]
    two, three = three_on(got, w, wn, far, we, z_ref, o_ref, b_ref, c_ref)
    for i in both:
        for n in range(3):
            e_ref[:, tile(5 - n if i else n)] = three[i][n]
    if not last:
        _, p_ref, zn_ref, _, _ = rest
        z, parts = prepare(w, three, [bf(y[2]) for y in three], two)
        for i in both:
            p_ref[:, tile(i)] = two[i][1]
            zn_ref[:, tile(i)] = z[i]
    if last:
        g = rest[0][...] + gram(e_ref[...])
        rest[2][...] = jnp.concatenate([g[: K // 2], g[K // 2 :]], axis=1)
    else:
        send(even, parts[0], parts[1], rest[3], rest[4])


def split(x):
    high = x.astype(BF16)
    rest = x - high.astype(F32)
    mid = rest.astype(BF16)
    return high, mid, (rest - mid.astype(F32)).astype(BF16)


def inverse_factor(g):
    row = lax.broadcasted_iota(jnp.int32, (K, K), 0)
    col = lax.broadcasted_iota(jnp.int32, (K, K), 1)
    whole = jnp.concatenate([g, (row == col).astype(F32)], axis=1)
    count = K // 8
    shape = (8, 2 * K)
    blocks = [whole[8 * i : 8 * i + 8] for i in range(count)]
    sub = lax.broadcasted_iota(jnp.int32, shape, 0)
    scaled = []
    for b in range(count):
        rows = [jnp.broadcast_to(blocks[b][a : a + 1], shape) for a in range(8)]
        entry = {
            (a, c): jnp.broadcast_to(rows[a][:, 8 * b + c : 8 * b + c + 1], shape)
            for a in range(8)
            for c in range(8)
        }
        columns = {
            i: [jnp.broadcast_to(blocks[i][:, 8 * b + c : 8 * b + c + 1], shape) for c in range(8)]
            for i in range(b + 1, count)
        }
        pivots, inverses = rows[0], None
        for a in range(8):
            inverse = 1.0 / entry[a, a]
            inverses = inverse if a == 0 else jnp.where(sub == a, inverse, inverses)
            if a > 0:
                pivots = jnp.where(sub == a, rows[a], pivots)
            for r in range(a + 1, 8):
                m = entry[r, a] * inverse
                rows[r] = rows[r] - m * rows[a]
                for c in range(a + 1, 8):
                    entry[r, c] = entry[r, c] - m * entry[a, c]
            for i in columns:
                m = columns[i][a] * inverse
                for c in range(a + 1, 8):
                    columns[i][c] = columns[i][c] - m * entry[a, c]
                columns[i][a] = m
        for i in columns:
            update = columns[i][0] * rows[0]
            for a in range(1, 8):
                update = update + columns[i][a] * rows[a]
            blocks[i] = blocks[i] - update
        scaled.append(pivots * jnp.sqrt(inverses))
    return jnp.concatenate(scaled, axis=0)[:, K:]


def whiten_kernel(scale, g_ref, e_ref, i_ref, out_ref, buf, sems):
    g = g_ref[...] * scale
    high, mid, low = split(inverse_factor(jnp.concatenate([g[:, :K], g[:, K:]], axis=0)))
    left = jnp.concatenate([high, mid, high, low, mid, high], axis=1)
    copies = []
    for n, (at, y) in enumerate(
        ((tile(0, 3), e_ref[:, tile(0, 3)]), (tile(3, 2), i_ref[...]), (tile(5, 3), e_ref[:, tile(3, 3)]))
    ):
        yh, ym, yl = split(y)
        right = jnp.concatenate([yh, yh, ym, yh, ym, yl], axis=0)
        buf[:, at] = dot(left, right)
        copy = pltpu.make_async_copy(buf.at[:, at], out_ref.at[:, at], sems.at[n])
        copy.start()
        copies.append(copy)
    for copy in copies:
        copy.wait()


def local(modes, tiles, tile_pair, boundary):
    count = lax.axis_size("slab") * lax.axis_size("col")
    pairs_even = [(i, i ^ 1) for i in range(count)]
    pairs_odd = [(i, (i + 1) % count if i % 2 else (i - 1) % count) for i in range(count)]

    def exchange(se, so):
        ro = lax.ppermute(so, AXES, pairs_odd)
        re = lax.ppermute(se, AXES, pairs_even)
        return re, ro

    def f32(tiles_wide):
        return pltpu.VMEM((K, tiles_wide * TB), F32)

    def weights(n):
        return pltpu.VMEM((n * TB, TB), BF16)

    def sends(rows):
        return pltpu.VMEM((rows, TB), BF16)

    w_out, w_edge, z, se, so, inv = pl.pallas_call(
        first_kernel,
        out_shape=(
            weights(4), weights(2), f32(2), sends(2 * K + TB), sends(2 * K + TB), pltpu.SMEM((TL,), jnp.int32),
        ),
        in_specs=[HBM, HBM, HBM, HBM],
        out_specs=(VM, VM, VM, VM, VM, SM),
        scratch_shapes=[
            pltpu.SMEM((TL,), jnp.int32),
            pltpu.SMEM((1, 2), jnp.int32),
            pltpu.VMEM((K, 4 * TB), F32),
            pltpu.SemaphoreType.DMA((8,)),
            pltpu.SemaphoreType.DMA((2,)),
        ],
        compiler_params=params(8),
        name="first",
    )(hbm(boundary), hbm(tile_pair), hbm(modes), hbm(tiles))
    re = lax.ppermute(se, AXES, pairs_even)
    ro = lax.ppermute(so, AXES, pairs_odd)
    w_in, j, m, b, o, fe, fo = pl.pallas_call(
        load_kernel,
        out_shape=(weights(18), f32(6), f32(4), f32(4), f32(2), weights(1), weights(1)),
        in_specs=[SM, HBM, HBM, VM, VM],
        out_specs=(VM,) * 7,
        scratch_shapes=[
            pltpu.VMEM((K, ROWS), F32),
            pltpu.VMEM((K, ROWS), BF16),
            pltpu.VMEM((K, 6 * TB), BF16),
            pltpu.SemaphoreType.DMA((18,)),
            pltpu.SemaphoreType.DMA,
        ],
        compiler_params=params(12),
        cost_estimate=cost(40),
        name="load",
    )(inv, hbm(modes), hbm(tiles), pin(w_out), pin(w_edge))
    fo, re = lax.optimization_barrier((fo, re))
    fe, fo = exchange(fe, fo)
    e, z, se, so, wn = pl.pallas_call(
        edge2_kernel,
        out_shape=(f32(4), f32(2), sends(3 * K), sends(3 * K), weights(2)),
        in_specs=[VM] * 9,
        out_specs=(VM,) * 5,
        compiler_params=params(8),
        name="edge2",
    )(re, ro, pin(z), pin(o), pin(b), pin(w_in), pin(w_out), pin(m), pin(j))
    state = (e, m, j)
    for later in (False, True):
        re, ro = exchange(se, so)
        outs = pl.pallas_call(
            functools.partial(step_kernel, later, later),
            out_shape=(f32(4), f32(4), f32(2), f32(2), f32(4)) + ((pltpu.VMEM((K, K), F32),) if later else ()),
            in_specs=[VM] * (len(state) + 3),
            out_specs=(VM,) * (6 if later else 5),
            scratch_shapes=[
                pltpu.VMEM((K, ROWS), BF16),
                pltpu.VMEM((K, 6 * TB), BF16),
                pltpu.VMEM((K, 4 * TB), BF16),
                pltpu.VMEM((K, 6 * TB), F32),
            ],
            compiler_params=params(10),
            cost_estimate=cost(52),
            name="step",
        )(*(pin(x) for x in state), pin(w_in), pin(w_out), pin(w_edge))
        m, b, o, t, c = outs[:5]
        shared = (
            re, ro, pin(z), pin(o), pin(b), pin(c), pin(w_in), pin(w_out), pin(wn), pin(w_edge), fe, fo
        )
        if not later:
            e, p, z, se, so = pl.pallas_call(
                functools.partial(edge3_kernel, False),
                out_shape=(f32(6), f32(2), f32(2), sends(3 * K), sends(3 * K)),
                in_specs=[VM] * 12,
                out_specs=(VM,) * 5,
                compiler_params=params(8),
                name="edge3",
            )(*shared)
            state = (e, t, p, m)
    e, g = pl.pallas_call(
        functools.partial(edge3_kernel, True),
        out_shape=(f32(6), pltpu.VMEM((K // 2, 2 * K), F32)),
        in_specs=[VM] * 13,
        out_specs=(VM, VM),
        compiler_params=params(8),
        name="final",
    )(*shared, pin(outs[5]))
    for group in ((16,), (1, 3, 2), (4, 12, 8), (32, 96, 64)):
        got = [lax.ppermute(g, AXES, [(i, i ^ bits) for i in range(count)]) for bits in group]
        for other in got:
            g = g + other
    return pl.pallas_call(
        functools.partial(whiten_kernel, 1.0 / (ROWS * count)),
        out_shape=jax.ShapeDtypeStruct((K, ROWS), F32),
        in_specs=[VM, VM, VM],
        out_specs=HBM,
        scratch_shapes=[pltpu.VMEM((K, ROWS), F32), pltpu.SemaphoreType.DMA((3,))],
        compiler_params=params(16),
        name="whiten",
    )(g, pin(e), pin(t))


def solution(mesh):
    placed = (
        P(None, AXES),
        P(AXES, None, None),
        P(AXES),
        P(AXES, None),
    )
    return jax.shard_map(
        local, mesh=mesh, in_specs=placed, out_specs=P(None, AXES), check_vma=False
    )
```
